32 devices in a mesh: grp: 4 (over x, core), rep: 8 (over z, y).
Axes of the slice: x: 2, y: 2, z: 4, core: 2. Of those that a mesh axis runs over, the one named last changes fastest.
Arguments:
- particles: bfloat16 [8192, 64, 256], P(('grp', 'rep')), may hold values from -6 to 6
- noise_var: float32 [8192], P(('grp', 'rep')), may hold values from 32 to 800
- references: bfloat16 [200, 64, 256], P('grp', 'rep'), may hold values from -6 to 6
- class_order: int32 [200], replicated, may hold values from 0 to 199, as said below
- candidates: int32 [32, 8], P(('grp', 'rep')), may hold values from 0 to 199, as said below
Outputs:
- class_sums: float32 [200, 64, 256], P('grp', 'rep')
- class_weights: float32 [200], P('grp')
The draws below stay inside these ranges and needn't reach their ends.
Inputs may be any that keep to these rules, and one draw needn't show every extreme that they name: `class_order`: a permutation; the slots of index g of grp are g * 50 to g * 50 + 49. `candidates`: each row names 8 different classes, whose slots lie with 4 indices of grp, exactly 2 with each.
All inputs are finite; a program needn't handle non-finite values.
Results may differ from the reference program's by a relative error of at most 0.0024.
Values may be sent and summed in bfloat16 or wider, within the bound.
A program may use at most 128 MiB of HBM per device.

```python
import math
import jax
import jax.numpy as jnp
from jax import lax

C = 200
R = 64
K = 128
CAND = 8
MOST_OWN = 2
B = 256
PARTICLES = 8192
BLOCKS = 32
CG = 50
N_GRP = 4


def shared_draw(key):
    order_perm = jax.random.permutation(jax.random.fold_in(key, 11), C).astype(jnp.int32)
    pairs = CAND // MOST_OWN
    key_one = jax.random.fold_in(key, 21)
    key_two = jax.random.fold_in(key, 22)
    key_three = jax.random.fold_in(key, 23)
    key_four = jax.random.fold_in(key, 24)
    key_five = jax.random.fold_in(key, 25)
    base_owner = jnp.minimum(jax.random.randint(key_one, (BLOCKS, 1), 0, N_GRP), jax.random.randint(key_two, (BLOCKS, 1), 0, N_GRP)).astype(jnp.int32)
    pair_index = jnp.arange(pairs, dtype=jnp.int32)[None, :]
    pair_owner = (base_owner + pair_index) % N_GRP
    first_slot = jnp.minimum(jax.random.randint(key_three, (BLOCKS, pairs), 0, CG), jax.random.randint(key_four, (BLOCKS, pairs), 0, CG)).astype(jnp.int32)
    step_slot = (1 + jax.random.randint(key_five, (BLOCKS, pairs), 0, CG - 1)).astype(jnp.int32)
    second_slot = (first_slot + step_slot) % CG
    within = jnp.stack([first_slot, second_slot], axis=2).reshape(BLOCKS, CAND)
    owners = jnp.repeat(pair_owner, MOST_OWN, axis=1)
    slot_ids = (owners * CG + within).astype(jnp.int32)
    return (order_perm, order_perm[slot_ids].astype(jnp.int32))


def draw_class_order(key, part):
    return shared_draw(key)[0]


def draw_candidates(key, part):
    return shared_draw(key)[1]


def shard_levels(key, shape, shards, low, largest):
    level = 1.0
    for position, blocks in shards:
        draws = jax.random.uniform(jax.random.fold_in(jax.random.fold_in(key, 6), position), (blocks,), jnp.float32, low / len(shards), largest / len(shards))
        level = level * jnp.repeat(jnp.exp(draws), shape[position] // blocks).reshape((-1,) + (1,) * (len(shape) - 1 - position))
    return level


def scatter_about(stream_key, extent, width, bound, split=(), kind=jnp.bfloat16):
    values = jax.random.normal(stream_key, extent, jnp.float32) * width
    if len(split) > 0:
        values = shard_levels(stream_key, extent, split, -0.22, 0.18) * values
    return jnp.clip(values, min=-bound, max=bound).astype(kind)


def setup_inputs(seed: int = 0) -> dict:
    streams_of = jax.random.split(jax.random.key(seed), 6)
    particles = scatter_about(streams_of[0], (PARTICLES, R, 2 * K), 1.0, 6.0, ((0, 32),))
    noise_var = jnp.clip(jnp.exp(math.log(800.0) - 3.218876 * jax.random.uniform(streams_of[1], (PARTICLES,), jnp.float32) ** shard_levels(streams_of[1], (PARTICLES,), ((0, 32),), -0.2, 0.2)), 32.0, 800.0)
    references = scatter_about(streams_of[2], (C, R, 2 * K), 1.0, 6.0, ((0, 4), (1, 8)))
    class_order = draw_class_order(jax.random.fold_in(streams_of[5], 71), 0)
    candidates = draw_candidates(jax.random.fold_in(streams_of[5], 71), 0)
    return dict(particles=particles, noise_var=noise_var, references=references, class_order=class_order, candidates=candidates)


precise = lax.Precision.HIGHEST


def angle_tables(freq_count, angle_count):
    freq_index = jnp.arange(freq_count, dtype=jnp.int32)[:, None]
    angle_index = jnp.arange(angle_count, dtype=jnp.int32)[None, :]
    phase_angle = ((freq_index * angle_index) % angle_count).astype(jnp.float32) * (2.0 * math.pi / angle_count)
    cosine_table = jnp.cos(phase_angle)
    sine_table = jnp.sin(phase_angle)
    to_angles = jnp.concatenate([cosine_table, -sine_table], axis=0)
    to_freqs = jnp.concatenate([cosine_table.T, sine_table.T], axis=1)
    return to_angles, to_freqs


def contract(pattern, left_side, right_side):
    return jnp.einsum(pattern, left_side.astype(jnp.float32), right_side.astype(jnp.float32), precision=precise)


def block_terms(block_rows, block_noise, chosen, to_angles, to_freqs):
    half_width = block_rows.shape[2] // 2
    row_count = block_rows.shape[0]
    cand_count = chosen.shape[0]
    angle_count = to_angles.shape[1]
    x_real, x_imag = block_rows[:, :, :half_width], block_rows[:, :, half_width:]
    r_real, r_imag = chosen[:, :, :half_width], chosen[:, :, half_width:]
    s_real = contract("prk,crk->pck", x_real, r_real) + contract("prk,crk->pck", x_imag, r_imag)
    s_imag = contract("prk,crk->pck", x_imag, r_real) - contract("prk,crk->pck", x_real, r_imag)
    spectra = jnp.concatenate([s_real, s_imag], axis=2)
    correlation = jnp.dot(spectra.reshape(-1, 2 * half_width), to_angles, precision=precise).reshape(row_count, cand_count, angle_count)
    chosen_wide = chosen.astype(jnp.float32)
    ref_norm = jnp.sum(chosen_wide * chosen_wide, axis=(1, 2))
    logits = (correlation - 0.5 * ref_norm[None, :, None]) / block_noise[:, None, None]
    row_max = jnp.max(logits, axis=(1, 2), keepdims=True)
    exponent = jnp.exp(logits - row_max)
    responsibility = exponent / jnp.sum(exponent, axis=(1, 2), keepdims=True)
    weight_spectra = jnp.dot(responsibility.reshape(-1, angle_count), to_freqs, precision=precise)
    weight_spectra = weight_spectra.reshape(row_count, cand_count, 2 * half_width).astype(jnp.bfloat16)
    w_real, w_imag = weight_spectra[:, :, :half_width], weight_spectra[:, :, half_width:]
    sum_real = contract("prk,pck->crk", x_real, w_real) - contract("prk,pck->crk", x_imag, w_imag)
    sum_imag = contract("prk,pck->crk", x_real, w_imag) + contract("prk,pck->crk", x_imag, w_real)
    numerator = jnp.concatenate([sum_real, sum_imag], axis=2)
    return numerator, jnp.sum(responsibility, axis=(0, 2))


def reference(particles, noise_var, references, class_order, candidates):
    to_angles, to_freqs = angle_tables(K, 2 * K)
    slot_index = jnp.arange(C, dtype=jnp.int32)
    block_data = particles.reshape(BLOCKS, B, R, 2 * K)
    noise_blocks = noise_var.reshape(BLOCKS, B)

    def advance(totals, inputs):
        block_rows, block_noise, block_cands = inputs
        slot_ids = jnp.sum(jnp.where(class_order[None, :] == block_cands[:, None], slot_index[None, :], 0), axis=1).astype(jnp.int32)
        chosen = jnp.take(references, slot_ids, axis=0)
        numerator, weight = block_terms(block_rows, block_noise, chosen, to_angles, to_freqs)
        sum_total, weight_total = totals
        sum_total = sum_total.at[slot_ids].add(numerator)
        weight_total = weight_total.at[slot_ids].add(weight)
        return (sum_total, weight_total), None

    initial = (jnp.zeros((C, R, 2 * K), jnp.float32), jnp.zeros((C,), jnp.float32))
    (class_sums, class_weights), _ = lax.scan(advance, initial, (block_data, noise_blocks, candidates))
    return (class_sums, class_weights)
```

```python
import functools
import math

import jax
import jax.numpy as jnp
import numpy as np
from jax import lax
from jax.experimental import pallas as pl
from jax.experimental.pallas import tpu as pltpu
from jax.sharding import PartitionSpec as P

precise = lax.Precision.HIGHEST
GROUP = 16
PITCH = GROUP + 4
OWN = 2


def angle_tables(freq_count, angle_count):
    product = np.arange(freq_count)[:, None] * np.arange(angle_count)[None, :] % angle_count
    phase_angle = product * (2.0 * math.pi / angle_count)
    return np.cos(phase_angle).astype(np.float32), np.sin(phase_angle).astype(np.float32)


def table_parts(table):
    high = table.astype(jnp.bfloat16)
    return high, (table - high.astype(np.float32)).astype(jnp.bfloat16)


def peer_of(step, n_rep, total):
    me = lax.axis_index("grp") * n_rep + lax.axis_index("rep")
    peer = lax.rem(me + step, total)
    return peer, {"grp": peer // n_rep, "rep": lax.rem(peer, n_rep)}


def greet_all(n_rep, total):
    barrier = pltpu.get_barrier_semaphore()

    @pl.loop(1, total)
    def _(step):
        _, where = peer_of(step, n_rep, total)
        pl.semaphore_signal(
            barrier, inc=1, device_id=where, device_id_type=pl.DeviceIdType.MESH
        )


def await_all(total):
    pl.semaphore_wait(pltpu.get_barrier_semaphore(), total - 1)


def remote(src, dst, send_sem, recv_sem, where):
    return pltpu.make_async_remote_copy(
        src_ref=src,
        dst_ref=dst,
        send_sem=send_sem,
        recv_sem=recv_sem,
        device_id=where,
        device_id_type=pl.DeviceIdType.MESH,
    )


def relayout_blocks(
    rows_ref, major_ref, in_buf, mid_buf, out_buf, in_sem, out_sem, start, stop
):
    half = rows_ref.shape[2] // 2

    def load(block):
        slot = lax.rem(block, 2)
        return pltpu.make_async_copy(
            rows_ref.at[pl.ds(block * GROUP, GROUP)], in_buf.at[slot], in_sem.at[slot]
        )

    def store(block):
        slot = lax.rem(block, 2)
        return pltpu.make_async_copy(
            out_buf.at[slot],
            major_ref.at[:, pl.ds(pl.multiple_of(block * GROUP, GROUP), GROUP), :],
            out_sem.at[slot],
        )

    load(start).start()

    @pl.loop(start, stop)
    def _(block):
        slot = lax.rem(block, 2)

        @pl.when(block + 1 < stop)
        def _():
            load(block + 1).start()

        load(block).wait()

        @pl.when(block >= start + 2)
        def _():
            store(block - 2).wait()

        for p in range(GROUP):
            both = jnp.concatenate(
                [in_buf[slot, p, :, :half], in_buf[slot, p, :, half:]], axis=0
            )
            mid_buf[pl.ds(p, half, stride=PITCH), :] = both.T.astype(jnp.float32)
        for k in range(half):
            out_buf[slot, k] = mid_buf[pl.ds(k * PITCH, GROUP), :].astype(out_buf.dtype)
        store(block).start()

    store(stop - 2).wait()
    store(stop - 1).wait()


def fetch_kernel(
    n_rep,
    total,
    cand_ref,
    order_ref,
    refs_ref,
    rows_ref,
    got_ref,
    slots_ref,
    major_ref,
    cand_pad,
    cand_all,
    slot_vec,
    slot_smem,
    send_buf,
    c_send,
    c_recv,
    d_send,
    d_recv,
    l_sem,
    in_buf,
    mid_buf,
    out_buf,
    in_sem,
    out_sem,
):
    grp = lax.axis_index("grp")
    me = grp * n_rep + lax.axis_index("rep")
    owned = refs_ref.shape[0]
    cand_pad[...] = jnp.full(cand_pad.shape, -1, jnp.int32)
    cand_pad[:, : cand_ref.shape[1]] = cand_ref[...]
    greet_all(n_rep, total)
    relayout = functools.partial(
        relayout_blocks, rows_ref, major_ref, in_buf, mid_buf, out_buf, in_sem, out_sem
    )
    blocks = rows_ref.shape[0] // GROUP
    cut_one, cut_two = blocks // 4, blocks // 2
    relayout(0, cut_one)
    await_all(total)

    def cand_copy(step, slot):
        _, where = peer_of(step, n_rep, total)
        return remote(cand_pad, cand_all.at[slot], c_send.at[step], c_recv.at[slot], where)

    @pl.loop(1, total)
    def _(step):
        cand_copy(step, me).start()

    cand_all[me] = cand_pad[...]
    relayout(cut_one, cut_two)

    @pl.loop(1, total)
    def _(step):
        cand_copy(step, peer_of(step, n_rep, total)[0]).wait_recv()

    order = order_ref[...]
    slot_no = lax.broadcasted_iota(jnp.int32, (1, order.shape[1]), 1) - grp * owned
    mine = jnp.where((slot_no >= 0) & (slot_no < owned), order, -2)
    cands = cand_all[...].reshape(total, cand_all.shape[2])
    hit = cands[:, 0:1] == mine
    for j in range(1, cand_ref.shape[1]):
        hit = jnp.logical_or(hit, cands[:, j : j + 1] == mine)
    first = jnp.min(jnp.where(hit, slot_no, 2 * owned), axis=1, keepdims=True)
    last = jnp.max(jnp.where(hit, slot_no, -1), axis=1, keepdims=True)
    lane = lax.broadcasted_iota(jnp.int32, slots_ref.shape, 1)
    slots_ref[...] = jnp.where(lane == 0, first, last)
    slot_vec[...] = jnp.where(
        lane == 0, jnp.minimum(first, owned - 1), jnp.maximum(last, 0)
    )
    to_scalar = pltpu.make_async_copy(slot_vec, slot_smem, l_sem.at[0])
    to_scalar.start()
    to_scalar.wait()

    def data_copy(step, block, slot):
        _, where = peer_of(step, n_rep, total)
        return remote(
            send_buf.at[block], got_ref.at[slot], d_send.at[step], d_recv.at[slot], where
        )

    @pl.loop(1, total)
    def _(step):
        peer, _ = peer_of(step, n_rep, total)
        for i in range(OWN):
            send_buf[peer, i] = refs_ref[slot_smem[peer, i]]
        data_copy(step, peer, me).start()

    for i in range(OWN):
        got_ref[me, i] = refs_ref[slot_smem[me, i]]

    relayout(cut_two, blocks)

    @pl.loop(1, total)
    def _(step):
        peer, _ = peer_of(step, n_rep, total)
        cand_copy(step, me).wait_send()
        data_copy(step, peer, peer).wait()


def fetch(cand, order, refs, rows, n_rep, total):
    count, depth, full = rows.shape
    half = full // 2
    owned, cycles, width = refs.shape
    vmem = pl.BlockSpec(memory_space=pltpu.VMEM)
    return pl.pallas_call(
        functools.partial(fetch_kernel, n_rep, total),
        out_shape=(
            jax.ShapeDtypeStruct((total, OWN, cycles, width), refs.dtype),
            jax.ShapeDtypeStruct((total, 128), jnp.int32),
            jax.ShapeDtypeStruct((half, count, 2 * depth), rows.dtype),
        ),
        in_specs=[vmem] * 3 + [pl.BlockSpec(memory_space=pl.ANY)],
        out_specs=(vmem, vmem, pl.BlockSpec(memory_space=pl.ANY)),
        scratch_shapes=[
            pltpu.VMEM((1, 128), jnp.int32),
            pltpu.VMEM((total, 1, 128), jnp.int32),
            pltpu.VMEM((total, 128), jnp.int32),
            pltpu.SMEM((total, 128), jnp.int32),
            pltpu.VMEM((total, OWN, cycles, width), refs.dtype),
            pltpu.SemaphoreType.DMA((total,)),
            pltpu.SemaphoreType.DMA((total,)),
            pltpu.SemaphoreType.DMA((total,)),
            pltpu.SemaphoreType.DMA((total,)),
            pltpu.SemaphoreType.DMA((1,)),
            pltpu.VMEM((2, GROUP, depth, full), rows.dtype),
            pltpu.VMEM((half * PITCH, 2 * depth), jnp.float32),
            pltpu.VMEM((2, half, GROUP, 2 * depth), rows.dtype),
            pltpu.SemaphoreType.DMA((2,)),
            pltpu.SemaphoreType.DMA((2,)),
        ],
        compiler_params=pltpu.CompilerParams(collective_id=0, has_side_effects=True),
        name="fetch",
    )(cand, order, refs, rows)


def return_kernel(
    n_rep, total, sums_ref, weight_ref, got_ref, got_w_ref, s_send, s_recv, w_send, w_recv, l_sem
):
    grp = lax.axis_index("grp")
    rep = lax.axis_index("rep")
    me = grp * n_rep + rep
    greet_all(n_rep, total)
    await_all(total)

    def copies(step, slot):
        _, where = peer_of(step, n_rep, total)
        return (
            remote(
                sums_ref.at[where["grp"], where["rep"]],
                got_ref.at[slot],
                s_send.at[step],
                s_recv.at[slot],
                where,
            ),
            remote(
                weight_ref.at[where["grp"]],
                got_w_ref.at[slot],
                w_send.at[step],
                w_recv.at[slot],
                where,
            ),
        )

    @pl.loop(1, total)
    def _(step):
        for copy in copies(step, me):
            copy.start()

    got_ref[me] = sums_ref[grp, rep]
    got_w_ref[me] = weight_ref[grp]

    @pl.loop(1, total)
    def _(step):
        for copy in copies(step, peer_of(step, n_rep, total)[0]):
            copy.wait()


def give_back(sums, weight, n_rep, total):
    vmem = pl.BlockSpec(memory_space=pltpu.VMEM)
    return pl.pallas_call(
        functools.partial(return_kernel, n_rep, total),
        out_shape=(
            jax.ShapeDtypeStruct((total,) + sums.shape[2:], sums.dtype),
            jax.ShapeDtypeStruct((total,) + weight.shape[1:], weight.dtype),
        ),
        in_specs=[vmem] * 2,
        out_specs=(vmem, vmem),
        scratch_shapes=[
            pltpu.SemaphoreType.DMA((total,)),
            pltpu.SemaphoreType.DMA((total,)),
            pltpu.SemaphoreType.DMA((total,)),
            pltpu.SemaphoreType.DMA((total,)),
            pltpu.SemaphoreType.DMA((1,)),
        ],
        compiler_params=pltpu.CompilerParams(collective_id=1, has_side_effects=True),
        name="give_back",
    )(sums, weight)


def split_wide(value):
    high = value.astype(jnp.bfloat16)
    return high, (value - high.astype(jnp.float32)).astype(jnp.bfloat16)


def dot_wide(left, right, precision=None):
    return jnp.dot(left, right, precision=precision, preferred_element_type=jnp.float32)


def terms_kernel(
    major_ref,
    q_ref,
    angles_high_ref,
    angles_low_ref,
    freqs_high_ref,
    freqs_low_ref,
    noise_ref,
    norm_ref,
    numer_ref,
    weight_ref,
    x_buf,
    f_buf,
    t_buf,
    x_sem,
):
    half, rows, depth = major_ref.shape
    both = q_ref.shape[1]
    cands = both // 2
    cycles = depth // 2
    chunks = x_sem.shape[0]
    span = half // chunks
    pitch = half + 4

    lanes = f_buf.shape[2]
    tiles = range(f_buf.shape[0])

    def spread(k):
        return pl.ds(k, both, stride=pitch)

    def take(part):
        return jnp.concatenate([f_buf[t, part, :] for t in tiles], axis=1)

    def put(part, value):
        for t in tiles:
            f_buf[t, part, :] = value[:, t * lanes : (t + 1) * lanes]

    def take_pair(j):
        return jnp.concatenate(
            [take(pl.ds((2 * j + c) * pitch, half)) for c in range(2)], axis=0
        )

    def put_pair(j, value):
        for c in range(2):
            put(pl.ds((2 * j + c) * pitch, half), value[c * half : (c + 1) * half])

    def chunk_copy(chunk):
        part = pl.ds(chunk * span, span)
        return pltpu.make_async_copy(major_ref.at[part], x_buf.at[part], x_sem.at[chunk])

    for chunk in range(chunks):
        chunk_copy(chunk).start()

    for chunk in range(chunks):
        chunk_copy(chunk).wait()

        @pl.loop(chunk * span, (chunk + 1) * span, unroll=8)
        def _(k):
            found = lax.dot_general(
                q_ref[k],
                x_buf[k],
                (((1,), (1,)), ((), ())),
                preferred_element_type=jnp.float32,
            )
            put(spread(k), found)

    inv_noise = 1.0 / noise_ref[...]
    top = jnp.full((1, rows), -jnp.inf, jnp.float32)
    for j in range(cands):
        high, low = split_wide(take_pair(j))
        correlation = (
            dot_wide(angles_high_ref[...], high)
            + dot_wide(angles_low_ref[...], high)
            + dot_wide(angles_high_ref[...], low)
        )
        logits = (correlation - norm_ref[j : j + 1, :]) * inv_noise
        put_pair(j, logits)
        top = jnp.maximum(top, jnp.max(logits, axis=0, keepdims=True))

    sums = []
    for j in range(cands):
        exponent = jnp.exp(take_pair(j) - top)
        put_pair(j, exponent)
        sums.append(jnp.sum(exponent, axis=0, keepdims=True))
    inv_sum = 1.0 / sum(sums)
    for j in range(cands):
        weight = jnp.sum(sums[j] * inv_sum, axis=1, keepdims=True)
        weight_ref[j : j + 1, :] = jnp.broadcast_to(weight, (1, weight_ref.shape[1]))
        high, low = split_wide(take_pair(j) * inv_sum)
        put_pair(
            j,
            dot_wide(freqs_high_ref[...], high)
            + dot_wide(freqs_low_ref[...], high)
            + dot_wide(freqs_high_ref[...], low),
        )

    @pl.loop(0, half, unroll=8)
    def _(k):
        spectra = take(spread(k)).astype(jnp.bfloat16)
        t_buf[spread(k), :] = dot_wide(spectra, x_buf[k])

    lane = lax.broadcasted_iota(jnp.int32, (half, depth), 1)
    for j in range(cands):
        by_real = t_buf[pl.ds(2 * j * pitch, half), :]
        by_imag = pltpu.roll(t_buf[pl.ds((2 * j + 1) * pitch, half), :], cycles, 1)
        pair = by_real + jnp.where(lane < cycles, -by_imag, by_imag)
        turned = pair.T.astype(jnp.bfloat16)
        numer_ref[j, :, :half] = turned[:cycles]
        numer_ref[j, :, half:] = turned[cycles:]


def block_terms(freq_major, noise, chosen):
    half, rows, depth = freq_major.shape
    cands, cycles, width = chosen.shape
    q_real, q_imag = chosen[:, :, :half], chosen[:, :, half:]
    q_both = jnp.stack(
        [
            jnp.concatenate([q_real, q_imag], axis=1),
            jnp.concatenate([-q_imag, q_real], axis=1),
        ],
        axis=1,
    )
    q_major = q_both.transpose(3, 0, 1, 2).reshape(half, 2 * cands, depth)
    cosine, sine = angle_tables(half, width)
    from_freqs = np.concatenate([cosine.T, -sine.T], axis=1)
    to_freqs = np.concatenate([cosine, sine], axis=0)
    wide = chosen.astype(jnp.float32)
    half_norm = 0.5 * jnp.sum(wide * wide, axis=(1, 2))
    half_norm = jnp.broadcast_to(half_norm[:, None], (cands, rows))
    vmem = pl.BlockSpec(memory_space=pltpu.VMEM)
    numerator, weight = pl.pallas_call(
        terms_kernel,
        out_shape=(
            jax.ShapeDtypeStruct((cands, cycles, width), jnp.bfloat16),
            jax.ShapeDtypeStruct((cands, 128), jnp.float32),
        ),
        in_specs=[pl.BlockSpec(memory_space=pltpu.HBM)] + [vmem] * 7,
        out_specs=(vmem, vmem),
        scratch_shapes=[
            pltpu.VMEM(freq_major.shape, freq_major.dtype),
            pltpu.VMEM((rows // 128, 2 * cands * (half + 4), 128), jnp.float32),
            pltpu.VMEM((2 * cands * (half + 4), depth), jnp.float32),
            pltpu.SemaphoreType.DMA((8,)),
        ],
        compiler_params=pltpu.CompilerParams(vmem_limit_bytes=52 * 2**20),
        name="terms",
    )(
        freq_major,
        q_major,
        *table_parts(from_freqs),
        *table_parts(to_freqs),
        noise.reshape(1, rows),
        half_norm,
    )
    return numerator, weight[:, 0]


def local(n_grp, n_rep, particles, noise_var, references, class_order, candidates):
    total = n_grp * n_rep
    cands = candidates.shape[1]
    owned, share, width = references.shape
    cycles = particles.shape[1]
    order = class_order.reshape(1, n_grp * owned)
    got, slots, freq_major = fetch(candidates, order, references, particles, n_rep, total)
    chosen = got.reshape(n_grp, n_rep, OWN, share, width).transpose(0, 2, 1, 3, 4)
    chosen = chosen.reshape(n_grp * OWN, cycles, width)
    spread = None
    if n_grp * OWN != cands:
        held = (class_order[:, None] == candidates.reshape(-1)[None, :]).any(axis=1)
        live = jnp.repeat(held.reshape(n_grp, owned).any(axis=1), OWN)
        place = jnp.cumsum(live.astype(jnp.int32)) - 1
        spread = (
            (place[None, :] == jnp.arange(cands)[:, None]) & live[None, :]
        ).astype(jnp.bfloat16)
        chosen = jnp.einsum(
            "js,srk->jrk", spread, chosen, preferred_element_type=jnp.float32
        ).astype(jnp.bfloat16)
    numerator, weight = block_terms(freq_major, noise_var, chosen)
    if spread is not None:
        numerator = jnp.einsum(
            "js,jrk->srk", spread, numerator, preferred_element_type=jnp.float32
        ).astype(jnp.bfloat16)
        weight = jnp.sum(spread.astype(jnp.float32) * weight[:, None], axis=0)
    parts = numerator.reshape(n_grp, OWN, n_rep, share, width).transpose(0, 2, 1, 3, 4)
    wide_weight = jnp.pad(weight.reshape(n_grp, 1, OWN), ((0, 0), (0, 0), (0, 128 - OWN)))
    back, back_weight = give_back(parts, wide_weight, n_rep, total)
    slot_of = slots[:, :OWN].reshape(-1)
    pick = jnp.arange(owned, dtype=jnp.int32)[:, None] == slot_of[None, :]
    class_sums = jnp.einsum(
        "sb,brk->srk",
        pick.astype(jnp.bfloat16),
        back.reshape(total * OWN, share, width),
        preferred_element_type=jnp.float32,
    )
    own_slot = jnp.arange(owned, dtype=jnp.int32)[:, None]
    class_weights = sum(
        jnp.sum(
            jnp.where(own_slot == slots[None, :, i], back_weight[None, :, 0, i], 0.0), axis=1
        )
        for i in range(OWN)
    )
    return class_sums, class_weights


def solution(mesh):
    placed = (
        P(("grp", "rep"), None, None),
        P(("grp", "rep")),
        P("grp", "rep", None),
        P(),
        P(("grp", "rep"), None),
    )
    return jax.shard_map(
        functools.partial(local, mesh.shape["grp"], mesh.shape["rep"]),
        mesh=mesh,
        in_specs=placed,
        out_specs=(P("grp", "rep", None), P("grp")),
        check_vma=False,
    )
```

```python
import functools
import math

import jax
import jax.numpy as jnp
import numpy as np
from jax import lax
from jax.experimental import pallas as pl
from jax.experimental.pallas import tpu as pltpu
from jax.sharding import PartitionSpec as P

GROUP = 16
PITCH = GROUP + 4
OWN = 2


def angle_tables(freq_count, angle_count):
    product = np.arange(freq_count)[:, None] * np.arange(angle_count)[None, :] % angle_count
    phase_angle = product * (2.0 * math.pi / angle_count)
    return np.cos(phase_angle).astype(np.float32), np.sin(phase_angle).astype(np.float32)


def table_parts(table):
    high = table.astype(jnp.bfloat16)
    return high, (table - high.astype(np.float32)).astype(jnp.bfloat16)


def peer_of(step, n_rep, total):
    me = lax.axis_index("grp") * n_rep + lax.axis_index("rep")
    peer = lax.rem(me + step, total)
    return peer, {"grp": peer // n_rep, "rep": lax.rem(peer, n_rep)}


def greet_all(n_rep, total):
    barrier = pltpu.get_barrier_semaphore()

    @pl.loop(1, total)
    def _(step):
        _, where = peer_of(step, n_rep, total)
        pl.semaphore_signal(
            barrier, inc=1, device_id=where, device_id_type=pl.DeviceIdType.MESH
        )


def await_all(total):
    pl.semaphore_wait(pltpu.get_barrier_semaphore(), total - 1)


def remote(src, dst, send_sem, recv_sem, where):
    return pltpu.make_async_remote_copy(
        src_ref=src,
        dst_ref=dst,
        send_sem=send_sem,
        recv_sem=recv_sem,
        device_id=where,
        device_id_type=pl.DeviceIdType.MESH,
    )


def split_wide(value):
    high = value.astype(jnp.bfloat16)
    return high, (value - high.astype(jnp.float32)).astype(jnp.bfloat16)


def dot_wide(left, right):
    return jnp.dot(left, right, preferred_element_type=jnp.float32)


def dot_parts(table_high, table_low, value):
    high, low = split_wide(value)
    return dot_wide(table_high, high) + dot_wide(table_low, high) + dot_wide(table_high, low)


def pass_kernel(
    n_rep,
    total,
    cand_ref,
    order_ref,
    noise_ref,
    angles_high_ref,
    angles_low_ref,
    freqs_high_ref,
    freqs_low_ref,
    refs_ref,
    rows_ref,
    sums_ref,
    class_weight_ref,
    cand_pad,
    cand_all,
    slot_vec,
    slot_smem,
    send_buf,
    got_buf,
    in_buf,
    mid_buf,
    x_buf,
    chosen_buf,
    q_buf,
    f_buf,
    t_buf,
    norm_buf,
    turned_buf,
    back_send,
    back_got,
    weight_send,
    weight_got,
    c_send,
    c_recv,
    d_send,
    d_recv,
    s_send,
    s_recv,
    w_send,
    w_recv,
    in_sem,
    l_sem,
):
    grp = lax.axis_index("grp")
    rep = lax.axis_index("rep")
    me = grp * n_rep + rep
    n_grp = total // n_rep
    owned, share, width = refs_ref.shape
    rows, cycles, _ = rows_ref.shape
    half = width // 2
    depth = 2 * cycles
    blocks = rows // GROUP
    cands = n_grp * OWN
    both = 2 * cands
    pitch = half + 4
    q_pitch = both + 4
    message = OWN * share

    def load(block):
        part = pl.ds(block * GROUP, GROUP)
        return pltpu.make_async_copy(rows_ref.at[part], in_buf.at[part], in_sem.at[block])

    @pl.loop(0, blocks)
    def _(block):
        load(block).start()

    cand_pad[...] = jnp.full(cand_pad.shape, -1, jnp.int32)
    cand_pad[:, : cand_ref.shape[1]] = cand_ref[...]
    greet_all(n_rep, total)

    def relayout(start, stop):
        @pl.loop(start, stop)
        def _(block):
            load(block).wait()
            for p in range(GROUP):
                image = in_buf.at[block * GROUP + p]
                turned = jnp.concatenate([image[:, :half], image[:, half:]], axis=0).T
                mid_buf[pl.ds(p, half, stride=PITCH), :] = turned.astype(jnp.float32)
            part = pl.ds(pl.multiple_of(block * GROUP, GROUP), GROUP)
            for k in range(half):
                x_buf[k, part, :] = mid_buf[pl.ds(k * PITCH, GROUP), :].astype(x_buf.dtype)

    cut_one, cut_two = blocks // 4, blocks // 2
    relayout(0, cut_one)
    await_all(total)

    def cand_copy(step, slot):
        _, where = peer_of(step, n_rep, total)
        return remote(cand_pad, cand_all.at[slot], c_send.at[step], c_recv.at[slot], where)

    @pl.loop(1, total)
    def _(step):
        cand_copy(step, me).start()

    cand_all[me] = cand_pad[...]
    relayout(cut_one, cut_two)

    @pl.loop(1, total)
    def _(step):
        cand_copy(step, peer_of(step, n_rep, total)[0]).wait_recv()

    order = order_ref[...]
    slot_no = lax.broadcasted_iota(jnp.int32, (1, order.shape[1]), 1) - grp * owned
    mine = jnp.where((slot_no >= 0) & (slot_no < owned), order, -2)
    wanted = cand_all[...].reshape(total, cand_all.shape[2])
    hit = wanted[:, 0:1] == mine
    for j in range(1, cand_ref.shape[1]):
        hit = jnp.logical_or(hit, wanted[:, j : j + 1] == mine)
    first = jnp.min(jnp.where(hit, slot_no, 2 * owned), axis=1, keepdims=True)
    last = jnp.max(jnp.where(hit, slot_no, -1), axis=1, keepdims=True)
    lane = lax.broadcasted_iota(jnp.int32, slot_vec.shape, 1)
    slot_vec[...] = jnp.where(
        lane == 0, jnp.minimum(first, owned - 1), jnp.maximum(last, 0)
    )
    to_scalar = pltpu.make_async_copy(slot_vec, slot_smem, l_sem.at[0])
    to_scalar.start()
    to_scalar.wait()

    def data_copy(step, block, slot):
        _, where = peer_of(step, n_rep, total)
        return remote(
            send_buf.at[block], got_buf.at[slot], d_send.at[step], d_recv.at[slot], where
        )

    @pl.loop(1, total)
    def _(step):
        peer, _ = peer_of(step, n_rep, total)
        for i in range(OWN):
            send_buf[peer, i] = refs_ref[slot_smem[peer, i]]
        data_copy(step, peer, me).start()

    for i in range(OWN):
        got_buf[me, i] = refs_ref[slot_smem[me, i]]

    relayout(cut_two, blocks)

    live = []
    if cands != cand_ref.shape[1]:
        held = cand_ref[:, 0:1] == order
        for j in range(1, cand_ref.shape[1]):
            held = jnp.logical_or(held, cand_ref[:, j : j + 1] == order)
        slot_all = lax.broadcasted_iota(jnp.int32, order.shape, 1)
        for g in range(n_grp):
            inside = held & (slot_all >= g * owned) & (slot_all < (g + 1) * owned)
            live.append(jnp.max(jnp.where(inside, 1.0, 0.0), axis=1, keepdims=True) > 0.0)

    @pl.loop(1, total)
    def _(step):
        peer, _ = peer_of(step, n_rep, total)
        cand_copy(step, me).wait_send()
        data_copy(step, peer, peer).wait()

    q_lane = lax.broadcasted_iota(jnp.int32, (half, depth), 1)
    for j in range(cands):
        g, i = j // OWN, j % OWN
        for r in range(n_rep):
            chosen_buf[j, pl.ds(r * share, share), :] = got_buf[g * n_rep + r, i].astype(
                jnp.float32
            )
        wide = chosen_buf[j]
        total_square = jnp.sum(jnp.sum(wide * wide, axis=0, keepdims=True), axis=1, keepdims=True)
        norm_buf[j : j + 1, :] = jnp.broadcast_to(0.5 * total_square, (1, rows))
        turned = jnp.concatenate([wide[:, :half], wide[:, half:]], axis=0).T
        q_buf[pl.ds(2 * j, half, stride=q_pitch), :] = turned
        rolled = pltpu.roll(turned, cycles, 1)
        q_buf[pl.ds(2 * j + 1, half, stride=q_pitch), :] = jnp.where(
            q_lane < cycles, -rolled, rolled
        )

    lanes = f_buf.shape[2]
    tiles = range(f_buf.shape[0])

    def spread(k):
        return pl.ds(k, both, stride=pitch)

    def take(part):
        return jnp.concatenate([f_buf[t, part, :] for t in tiles], axis=1)

    def put(part, value):
        for t in tiles:
            f_buf[t, part, :] = value[:, t * lanes : (t + 1) * lanes]

    def take_pair(j):
        return jnp.concatenate(
            [take(pl.ds((2 * j + c) * pitch, half)) for c in range(2)], axis=0
        )

    def put_pair(j, value):
        for c in range(2):
            put(pl.ds((2 * j + c) * pitch, half), value[c * half : (c + 1) * half])

    @pl.loop(0, half, unroll=8)
    def _(k):
        found = lax.dot_general(
            q_buf[pl.ds(k * q_pitch, both), :].astype(jnp.bfloat16),
            x_buf[k],
            (((1,), (1,)), ((), ())),
            preferred_element_type=jnp.float32,
        )
        put(spread(k), found)

    inv_noise = 1.0 / noise_ref[...]
    top = jnp.full((1, rows), -jnp.inf, jnp.float32)
    for j in range(cands):
        correlation = dot_parts(angles_high_ref[...], angles_low_ref[...], take_pair(j))
        logits = (correlation - norm_buf[j : j + 1, :]) * inv_noise
        if live:
            logits = jnp.where(live[j // OWN], logits, -jnp.inf)
        put_pair(j, logits)
        top = jnp.maximum(top, jnp.max(logits, axis=0, keepdims=True))

    sums = []
    for j in range(cands):
        exponent = jnp.exp(take_pair(j) - top)
        put_pair(j, exponent)
        sums.append(jnp.sum(exponent, axis=0, keepdims=True))
    inv_sum = 1.0 / sum(sums)
    w_lane = lax.broadcasted_iota(jnp.int32, (1, weight_send.shape[2]), 1)
    for g in range(n_grp):
        line = jnp.zeros(w_lane.shape, jnp.float32)
        for i in range(OWN):
            weight = jnp.sum(sums[g * OWN + i] * inv_sum, axis=1, keepdims=True)
            line = jnp.where(w_lane == i, weight, line)
        weight_send[g] = line

    def weight_copy(step, slot):
        _, where = peer_of(step, n_rep, total)
        return remote(
            weight_send.at[where["grp"]],
            weight_got.at[slot],
            w_send.at[step],
            w_recv.at[slot],
            where,
        )

    @pl.loop(1, total)
    def _(step):
        weight_copy(step, me).start()

    weight_got[me] = weight_send[grp]

    for j in range(cands):
        put_pair(
            j, dot_parts(freqs_high_ref[...], freqs_low_ref[...], take_pair(j) * inv_sum)
        )

    @pl.loop(0, half, unroll=8)
    def _(k):
        spectra = take(spread(k)).astype(jnp.bfloat16)
        t_buf[spread(k), :] = dot_wide(spectra, x_buf[k])

    def back_copy(g, r, slot):
        where = {"grp": g, "rep": r}
        peer = g * n_rep + r
        return remote(
            back_send.at[peer], back_got.at[slot], s_send.at[peer], s_recv.at[slot], where
        )

    for d in range(n_grp):
        g = lax.rem(grp + d, n_grp)
        for i in range(OWN):
            base = (g * OWN + i) * 2 * pitch
            by_real = t_buf[pl.ds(base, half), :]
            by_imag = pltpu.roll(t_buf[pl.ds(base + pitch, half), :], cycles, 1)
            turned = (by_real + jnp.where(q_lane < cycles, -by_imag, by_imag)).T
            for c in range(2):
                for r in range(n_rep):
                    at = c * cycles + r * share
                    turned_buf[
                        d, pl.ds(r * message + i * share, share), c * half : (c + 1) * half
                    ] = turned[at : at + share]
        for r in range(n_rep):
            back_send[g * n_rep + r] = turned_buf[d, pl.ds(r * message, message), :].astype(
                back_send.dtype
            )

        @pl.loop(0 if d else 1, n_rep)
        def _(step):
            back_copy(g, lax.rem(rep + step, n_rep), me).start()

    back_got[me] = back_send[me]

    shift = share.bit_length() - 1
    pick_row = lax.broadcasted_iota(jnp.int32, (owned * share, total * message), 0)
    pick_lane = lax.broadcasted_iota(jnp.int32, (owned * share, total * message), 1)
    member = lax.broadcasted_iota(jnp.int32, (total, total * message), 1) // share
    block_no = lax.broadcasted_iota(jnp.int32, (total, total * message), 0)
    of_member = jnp.where(member == block_no * OWN, first, 0)
    for i in range(1, OWN):
        of_member = of_member + jnp.where(member == block_no * OWN + i, last, 0)
    of_member = jnp.sum(of_member, axis=0, keepdims=True)
    fits = jnp.logical_and(
        lax.shift_right_logical(pick_row, shift) == of_member,
        ((pick_row ^ pick_lane) & (share - 1)) == 0,
    )
    pick = jnp.where(fits, 1.0, 0.0).astype(jnp.bfloat16)

    @pl.loop(1, total)
    def _(step):
        weight_copy(step, peer_of(step, n_rep, total)[0]).wait()

    got_weight = weight_got[...].reshape(total, weight_got.shape[2])
    w_slot = lax.broadcasted_iota(jnp.int32, got_weight.shape, 1)
    placed = jnp.where(w_slot == first, got_weight[:, 0:1], 0.0)
    placed = placed + jnp.where(w_slot == last, got_weight[:, 1:2], 0.0)
    class_weight_ref[...] = jnp.sum(placed, axis=0, keepdims=True)[:, :owned]

    @pl.loop(1, total)
    def _(step):
        peer, where = peer_of(step, n_rep, total)
        remote(
            back_send.at[peer], back_got.at[peer], s_send.at[peer], s_recv.at[peer], where
        ).wait()

    if message % 16 == 0:
        back = back_got[...].reshape(total * message, width)
    else:
        back = jnp.concatenate(
            [back_got[b].astype(jnp.float32) for b in range(total)], axis=0
        ).astype(jnp.bfloat16)
    sums_ref[...] = dot_wide(pick, back)


def local(n_grp, n_rep, particles, noise_var, references, class_order, candidates):
    total = n_grp * n_rep
    owned, share, width = references.shape
    rows, cycles, _ = particles.shape
    half = width // 2
    depth = 2 * cycles
    cands = n_grp * OWN
    message = OWN * share
    cosine, sine = angle_tables(half, width)
    from_freqs = np.concatenate([cosine.T, -sine.T], axis=1)
    to_freqs = np.concatenate([cosine, sine], axis=0)
    vmem = pl.BlockSpec(memory_space=pltpu.VMEM)
    dma = pltpu.SemaphoreType.DMA
    class_sums, class_weights = pl.pallas_call(
        functools.partial(pass_kernel, n_rep, total),
        out_shape=(
            jax.ShapeDtypeStruct((owned * share, width), jnp.float32),
            jax.ShapeDtypeStruct((1, owned), jnp.float32),
        ),
        in_specs=[vmem] * 8 + [pl.BlockSpec(memory_space=pltpu.HBM)],
        out_specs=(vmem, vmem),
        scratch_shapes=[
            pltpu.VMEM((1, 128), jnp.int32),
            pltpu.VMEM((total, 1, 128), jnp.int32),
            pltpu.VMEM((total, 128), jnp.int32),
            pltpu.SMEM((total, 128), jnp.int32),
            pltpu.VMEM((total, OWN, share, width), references.dtype),
            pltpu.VMEM((total, OWN, share, width), references.dtype),
            pltpu.VMEM(particles.shape, particles.dtype),
            pltpu.VMEM((half * PITCH, depth), jnp.float32),
            pltpu.VMEM((half, rows, depth), particles.dtype),
            pltpu.VMEM((cands, cycles, width), jnp.float32),
            pltpu.VMEM((half * (2 * cands + 4), depth), jnp.float32),
            pltpu.VMEM((rows // 128, 2 * cands * (half + 4), 128), jnp.float32),
            pltpu.VMEM((2 * cands * (half + 4), depth), jnp.float32),
            pltpu.VMEM((cands, rows), jnp.float32),
            pltpu.VMEM((n_grp, n_rep * message, width), jnp.float32),
            pltpu.VMEM((total, message, width), jnp.bfloat16),
            pltpu.VMEM((total, message, width), jnp.bfloat16),
            pltpu.VMEM((n_grp, 1, 128), jnp.float32),
            pltpu.VMEM((total, 1, 128), jnp.float32),
        ]
        + [dma((total,))] * 8
        + [dma((rows // GROUP,)), dma((1,))],
        compiler_params=pltpu.CompilerParams(
            collective_id=0, has_side_effects=True, vmem_limit_bytes=56 * 2**20
        ),
        name="em",
    )(
        candidates,
        class_order.reshape(1, n_grp * owned),
        noise_var.reshape(1, rows),
        *table_parts(from_freqs),
        *table_parts(to_freqs),
        references,
        particles,
    )
    return class_sums.reshape(owned, share, width), class_weights.reshape(owned)


def solution(mesh):
    placed = (
        P(("grp", "rep"), None, None),
        P(("grp", "rep")),
        P("grp", "rep", None),
        P(),
        P(("grp", "rep"), None),
    )
    return jax.shard_map(
        functools.partial(local, mesh.shape["grp"], mesh.shape["rep"]),
        mesh=mesh,
        in_specs=placed,
        out_specs=(P("grp", "rep", None), P("grp")),
        check_vma=False,
    )
```

```python
import functools
import math

import jax
import jax.numpy as jnp
import numpy as np
from jax import lax
from jax.experimental import pallas as pl
from jax.experimental.pallas import tpu as pltpu
from jax.sharding import PartitionSpec as P

GROUP = 16
PITCH = GROUP + 4
OWN = 2
LIMIT = 40


def angle_tables(freq_count, angle_count):
    product = np.arange(freq_count)[:, None] * np.arange(angle_count)[None, :] % angle_count
    phase_angle = product * (2.0 * math.pi / angle_count)
    return np.cos(phase_angle).astype(np.float32), np.sin(phase_angle).astype(np.float32)


def table_parts(table):
    high = table.astype(jnp.bfloat16)
    return high, (table - high.astype(np.float32)).astype(jnp.bfloat16)


def far_first(rep, n_rep, step):
    near = jnp.where(2 * rep < n_rep, rep, n_rep - 1 - rep)
    turn = step - (n_rep - 1 - 2 * near)
    inner = jnp.where(turn % 2 == 0, turn // 2, 2 * near - turn // 2)
    target = jnp.where(turn < 0, n_rep - 1 - step, inner)
    return jnp.where(2 * rep < n_rep, target, n_rep - 1 - target)


def each_peer(n_rep, n_grp, action):
    grp = lax.axis_index("grp")
    rep = lax.axis_index("rep")

    @pl.loop(0, n_rep)
    def _(step):
        to_rep = far_first(rep, n_rep, step)
        for ahead in range(n_grp - 1, -1, -1):
            to_grp = lax.rem(grp + ahead, n_grp)
            if ahead:
                action(to_grp, to_rep)
            else:

                @pl.when(to_rep != rep)
                def _():
                    action(to_grp, to_rep)


def peer_of(step, n_rep, total):
    me = lax.axis_index("grp") * n_rep + lax.axis_index("rep")
    peer = lax.rem(me + step, total)
    return peer, {"grp": peer // n_rep, "rep": lax.rem(peer, n_rep)}


def greet_all(n_rep, n_grp):
    barrier = pltpu.get_barrier_semaphore()

    def greet(to_grp, to_rep):
        pl.semaphore_signal(
            barrier,
            inc=1,
            device_id={"grp": to_grp, "rep": to_rep},
            device_id_type=pl.DeviceIdType.MESH,
        )

    each_peer(n_rep, n_grp, greet)


def await_all(total):
    pl.semaphore_wait(pltpu.get_barrier_semaphore(), total - 1)


def remote(src, dst, send_sem, recv_sem, where):
    return pltpu.make_async_remote_copy(
        src_ref=src,
        dst_ref=dst,
        send_sem=send_sem,
        recv_sem=recv_sem,
        device_id=where,
        device_id_type=pl.DeviceIdType.MESH,
    )


def split_wide(value):
    high = value.astype(jnp.bfloat16)
    return high, (value - high.astype(jnp.float32)).astype(jnp.bfloat16)


def dot_wide(left, right):
    return jnp.dot(left, right, preferred_element_type=jnp.float32)


def dot_parts(table_high, table_low, value):
    high, low = split_wide(value)
    return dot_wide(table_high, high) + dot_wide(table_low, high) + dot_wide(table_high, low)


def pass_kernel(
    n_rep,
    total,
    cand_hbm,
    order_hbm,
    noise_hbm,
    tables_hbm,
    refs_hbm,
    rows_ref,
    back_got,
    weight_got,
    slots_ref,
    cand_ref,
    order_ref,
    noise_ref,
    tables_ref,
    refs_ref,
    cand_pad,
    cand_all,
    slot_vec,
    slot_smem,
    send_buf,
    got_buf,
    in_buf,
    mid_buf,
    x_buf,
    chosen_buf,
    q_buf,
    f_buf,
    t_buf,
    norm_buf,
    turned_buf,
    back_send,
    weight_send,
    c_send,
    c_recv,
    d_send,
    d_recv,
    s_send,
    s_recv,
    w_send,
    w_recv,
    in_sem,
    l_sem,
):
    grp = lax.axis_index("grp")
    rep = lax.axis_index("rep")
    me = grp * n_rep + rep
    n_grp = total // n_rep
    owned, share, width = refs_ref.shape
    rows, cycles, _ = rows_ref.shape
    half = width // 2
    depth = 2 * cycles
    blocks = rows // GROUP
    cands = n_grp * OWN
    both = 2 * cands
    pitch = half + 4
    q_pitch = both + 4
    message = OWN * share

    def load(block):
        part = pl.ds(block * GROUP, GROUP)
        return pltpu.make_async_copy(rows_ref.at[part], in_buf.at[part], in_sem.at[block])

    pairs = (
        (cand_hbm, cand_ref),
        (order_hbm, order_ref),
        (refs_hbm, refs_ref),
        (noise_hbm, noise_ref),
        (tables_hbm, tables_ref),
    )
    reads = [
        pltpu.make_async_copy(src, dst, l_sem.at[n]) for n, (src, dst) in enumerate(pairs)
    ]
    reads[0].start()
    greet_all(n_rep, n_grp)
    for read in reads[1:3]:
        read.start()

    @pl.loop(0, blocks)
    def _(block):
        load(block).start()

    for read in reads[3:]:
        read.start()
    cand_pad[...] = jnp.full(cand_pad.shape, -1, jnp.int32)
    reads[0].wait()
    cand_pad[:, : cand_ref.shape[1]] = cand_ref[...]

    def relayout(start, stop):
        @pl.loop(start, stop)
        def _(block):
            load(block).wait()
            for p in range(GROUP):
                image = in_buf.at[block * GROUP + p]
                turned = jnp.concatenate([image[:, :half], image[:, half:]], axis=0).T
                mid_buf[pl.ds(p, half, stride=PITCH), :] = turned.astype(jnp.float32)
            part = pl.ds(pl.multiple_of(block * GROUP, GROUP), GROUP)
            for k in range(half):
                x_buf[k, part, :] = mid_buf[pl.ds(k * PITCH, GROUP), :].astype(x_buf.dtype)

    cut_one, cut_two = blocks // 4, blocks // 2
    relayout(0, cut_one)
    await_all(total)

    def cand_copy(to_grp, to_rep, slot):
        where = {"grp": to_grp, "rep": to_rep}
        peer = to_grp * n_rep + to_rep
        return remote(cand_pad, cand_all.at[slot], c_send.at[peer], c_recv.at[slot], where)

    each_peer(n_rep, n_grp, lambda g, r: cand_copy(g, r, me).start())

    cand_all[me] = cand_pad[...]
    relayout(cut_one, cut_two)

    @pl.loop(1, total)
    def _(step):
        peer, where = peer_of(step, n_rep, total)
        cand_copy(where["grp"], where["rep"], peer).wait_recv()

    reads[1].wait()
    reads[2].wait()
    order = order_ref[...]
    slot_no = lax.broadcasted_iota(jnp.int32, (1, order.shape[1]), 1) - grp * owned
    mine = jnp.where((slot_no >= 0) & (slot_no < owned), order, -2)
    wanted = cand_all[...].reshape(total, cand_all.shape[2])
    hit = wanted[:, 0:1] == mine
    for j in range(1, cand_ref.shape[1]):
        hit = jnp.logical_or(hit, wanted[:, j : j + 1] == mine)
    first = jnp.min(jnp.where(hit, slot_no, 2 * owned), axis=1, keepdims=True)
    last = jnp.max(jnp.where(hit, slot_no, -1), axis=1, keepdims=True)
    lane = lax.broadcasted_iota(jnp.int32, slot_vec.shape, 1)
    slot_vec[...] = jnp.where(
        lane == 0, jnp.minimum(first, owned - 1), jnp.maximum(last, 0)
    )
    to_scalar = pltpu.make_async_copy(slot_vec, slot_smem, l_sem.at[len(pairs)])
    to_scalar.start()
    to_scalar.wait()

    def data_copy(to_grp, to_rep, slot):
        where = {"grp": to_grp, "rep": to_rep}
        peer = to_grp * n_rep + to_rep
        return remote(
            send_buf.at[peer], got_buf.at[slot], d_send.at[peer], d_recv.at[slot], where
        )

    def give(to_grp, to_rep):
        peer = to_grp * n_rep + to_rep
        for i in range(OWN):
            send_buf[peer, i] = refs_ref[slot_smem[peer, i]]
        data_copy(to_grp, to_rep, me).start()

    each_peer(n_rep, n_grp, give)
    slots_ref[...] = jnp.where(lane == 0, first, last)

    for i in range(OWN):
        got_buf[me, i] = refs_ref[slot_smem[me, i]]

    relayout(cut_two, blocks)

    live = []
    if cands != cand_ref.shape[1]:
        held = cand_ref[:, 0:1] == order
        for j in range(1, cand_ref.shape[1]):
            held = jnp.logical_or(held, cand_ref[:, j : j + 1] == order)
        slot_all = lax.broadcasted_iota(jnp.int32, order.shape, 1)
        for g in range(n_grp):
            inside = held & (slot_all >= g * owned) & (slot_all < (g + 1) * owned)
            live.append(jnp.max(jnp.where(inside, 1.0, 0.0), axis=1, keepdims=True) > 0.0)

    @pl.loop(1, total)
    def _(step):
        peer, where = peer_of(step, n_rep, total)
        cand_copy(where["grp"], where["rep"], me).wait_send()
        data_copy(where["grp"], where["rep"], peer).wait()

    q_lane = lax.broadcasted_iota(jnp.int32, (half, depth), 1)
    for j in range(cands):
        g, i = j // OWN, j % OWN
        for r in range(n_rep):
            chosen_buf[j, pl.ds(r * share, share), :] = got_buf[g * n_rep + r, i].astype(
                jnp.float32
            )
        wide = chosen_buf[j]
        total_square = jnp.sum(jnp.sum(wide * wide, axis=0, keepdims=True), axis=1, keepdims=True)
        norm_buf[j : j + 1, :] = jnp.broadcast_to(0.5 * total_square, (1, rows))
        turned = jnp.concatenate([wide[:, :half], wide[:, half:]], axis=0).T
        q_buf[pl.ds(2 * j, half, stride=q_pitch), :] = turned
        rolled = pltpu.roll(turned, cycles, 1)
        q_buf[pl.ds(2 * j + 1, half, stride=q_pitch), :] = jnp.where(
            q_lane < cycles, -rolled, rolled
        )

    lanes = f_buf.shape[2]
    tiles = range(f_buf.shape[0])

    def spread(k):
        return pl.ds(k, both, stride=pitch)

    def take(part):
        return jnp.concatenate([f_buf[t, part, :] for t in tiles], axis=1)

    def put(part, value):
        for t in tiles:
            f_buf[t, part, :] = value[:, t * lanes : (t + 1) * lanes]

    def take_pair(j):
        return jnp.concatenate(
            [take(pl.ds((2 * j + c) * pitch, half)) for c in range(2)], axis=0
        )

    def put_pair(j, value):
        for c in range(2):
            put(pl.ds((2 * j + c) * pitch, half), value[c * half : (c + 1) * half])

    @pl.loop(0, half, unroll=8)
    def _(k):
        found = lax.dot_general(
            q_buf[pl.ds(k * q_pitch, both), :].astype(jnp.bfloat16),
            x_buf[k],
            (((1,), (1,)), ((), ())),
            preferred_element_type=jnp.float32,
        )
        put(spread(k), found)

    reads[3].wait()
    reads[4].wait()
    inv_noise = 1.0 / noise_ref[...]
    top = jnp.full((1, rows), -jnp.inf, jnp.float32)
    for j in range(cands):
        correlation = dot_parts(tables_ref[0], tables_ref[1], take_pair(j))
        logits = (correlation - norm_buf[j : j + 1, :]) * inv_noise
        if live:
            logits = jnp.where(live[j // OWN], logits, -jnp.inf)
        put_pair(j, logits)
        top = jnp.maximum(top, jnp.max(logits, axis=0, keepdims=True))

    sums = []
    for j in range(cands):
        exponent = jnp.exp(take_pair(j) - top)
        put_pair(j, exponent)
        sums.append(jnp.sum(exponent, axis=0, keepdims=True))
    inv_sum = 1.0 / sum(sums)
    w_lane = lax.broadcasted_iota(jnp.int32, (1, weight_send.shape[2]), 1)
    for g in range(n_grp):
        line = jnp.zeros(w_lane.shape, jnp.float32)
        for i in range(OWN):
            weight = jnp.sum(sums[g * OWN + i] * inv_sum, axis=1, keepdims=True)
            line = jnp.where(w_lane == i, weight, line)
        weight_send[g] = line

    def weight_copy(to_grp, to_rep, slot):
        where = {"grp": to_grp, "rep": to_rep}
        peer = to_grp * n_rep + to_rep
        return remote(
            weight_send.at[to_grp], weight_got.at[slot], w_send.at[peer], w_recv.at[slot], where
        )

    each_peer(n_rep, n_grp, lambda g, r: weight_copy(g, r, me).start())

    weight_got[me] = weight_send[grp]

    for j in range(cands):
        put_pair(j, dot_parts(tables_ref[2], tables_ref[3], take_pair(j) * inv_sum))

    @pl.loop(0, half, unroll=8)
    def _(k):
        spectra = take(spread(k)).astype(jnp.bfloat16)
        t_buf[spread(k), :] = dot_wide(spectra, x_buf[k])

    def back_copy(g, r, slot):
        where = {"grp": g, "rep": r}
        peer = g * n_rep + r
        return remote(
            back_send.at[peer], back_got.at[slot], s_send.at[peer], s_recv.at[slot], where
        )

    for d in range(n_grp):
        g = lax.rem(grp + d, n_grp)
        for i in range(OWN):
            base = (g * OWN + i) * 2 * pitch
            by_real = t_buf[pl.ds(base, half), :]
            by_imag = pltpu.roll(t_buf[pl.ds(base + pitch, half), :], cycles, 1)
            turned = (by_real + jnp.where(q_lane < cycles, -by_imag, by_imag)).T
            for c in range(2):
                for r in range(n_rep):
                    at = c * cycles + r * share
                    turned_buf[
                        d, pl.ds(r * message + i * share, share), c * half : (c + 1) * half
                    ] = turned[at : at + share]
        for r in range(n_rep):
            back_send[g * n_rep + r] = turned_buf[d, pl.ds(r * message, message), :].astype(
                back_send.dtype
            )

    each_peer(n_rep, n_grp, lambda g, r: back_copy(g, r, me).start())
    back_got[me] = back_send[me]

    @pl.loop(1, total)
    def _(step):
        peer, where = peer_of(step, n_rep, total)
        weight_copy(where["grp"], where["rep"], peer).wait()
        back_copy(where["grp"], where["rep"], peer).wait()


def place_kernel(
    share, back_ref, weight_ref, slots_ref, sums_hbm, class_weight_ref, sums_buf, out_sem
):
    total, message, width = back_ref.shape
    height = sums_buf.shape[0]
    owned = class_weight_ref.shape[1]
    chunks = out_sem.shape[0]
    shift = share.bit_length() - 1
    slots = slots_ref[...]
    member = lax.broadcasted_iota(jnp.int32, (total, total * message), 1)
    member = lax.shift_right_logical(member, shift)
    block_no = lax.broadcasted_iota(jnp.int32, (total, total * message), 0)
    of_member = jnp.zeros(member.shape, jnp.int32)
    for i in range(OWN):
        of_member = jnp.where(member == block_no * OWN + i, slots[:, i : i + 1], of_member)
    of_member = jnp.sum(of_member, axis=0, keepdims=True)
    if message % 16 == 0:
        back = back_ref[...].reshape(total * message, width)
    else:
        back = jnp.concatenate(
            [back_ref[b].astype(jnp.float32) for b in range(total)], axis=0
        ).astype(jnp.bfloat16)
    rows = height // chunks
    copies = []
    for chunk in range(chunks):
        part = pl.ds(chunk * rows, rows)
        row = lax.broadcasted_iota(jnp.int32, (rows, total * message), 0) + chunk * rows
        lane = lax.broadcasted_iota(jnp.int32, (rows, total * message), 1)
        fits = jnp.logical_and(
            lax.shift_right_logical(row, shift) == of_member,
            ((row ^ lane) & (share - 1)) == 0,
        )
        sums_buf[part, :] = dot_wide(jnp.where(fits, 1.0, 0.0).astype(jnp.bfloat16), back)
        copy = pltpu.make_async_copy(
            sums_buf.at[part], sums_hbm.at[part], out_sem.at[chunk]
        )
        copy.start()
        copies.append(copy)

    got_weight = weight_ref[...].reshape(total, weight_ref.shape[2])
    w_slot = lax.broadcasted_iota(jnp.int32, got_weight.shape, 1)
    placed = jnp.zeros(got_weight.shape, jnp.float32)
    for i in range(OWN):
        placed = placed + jnp.where(
            w_slot == slots[:, i : i + 1], got_weight[:, i : i + 1], 0.0
        )
    class_weight_ref[...] = jnp.sum(placed, axis=0, keepdims=True)[:, :owned]
    for copy in copies:
        copy.wait()


def local(n_grp, n_rep, particles, noise_var, references, class_order, candidates):
    total = n_grp * n_rep
    owned, share, width = references.shape
    rows, cycles, _ = particles.shape
    half = width // 2
    depth = 2 * cycles
    cands = n_grp * OWN
    message = OWN * share
    cosine, sine = angle_tables(half, width)
    from_freqs = np.concatenate([cosine.T, -sine.T], axis=1)
    to_freqs = np.concatenate([cosine, sine], axis=0)
    vmem = pl.BlockSpec(memory_space=pltpu.VMEM)
    dma = pltpu.SemaphoreType.DMA
    hbm = pl.BlockSpec(memory_space=pltpu.HBM)
    tables = jnp.stack([*table_parts(from_freqs), *table_parts(to_freqs)])
    back, weights, slots = pl.pallas_call(
        functools.partial(pass_kernel, n_rep, total),
        out_shape=(
            jax.ShapeDtypeStruct((total, message, width), jnp.bfloat16),
            jax.ShapeDtypeStruct((total, 1, 128), jnp.float32),
            jax.ShapeDtypeStruct((total, 128), jnp.int32),
        ),
        in_specs=[hbm] * 6,
        out_specs=(vmem, vmem, vmem),
        scratch_shapes=[
            pltpu.VMEM(candidates.shape, jnp.int32),
            pltpu.VMEM((1, n_grp * owned), jnp.int32),
            pltpu.VMEM((1, rows), jnp.float32),
            pltpu.VMEM((4, width, width), jnp.bfloat16),
            pltpu.VMEM(references.shape, references.dtype),
            pltpu.VMEM((1, 128), jnp.int32),
            pltpu.VMEM((total, 1, 128), jnp.int32),
            pltpu.VMEM((total, 128), jnp.int32),
            pltpu.SMEM((total, 128), jnp.int32),
            pltpu.VMEM((total, OWN, share, width), references.dtype),
            pltpu.VMEM((total, OWN, share, width), references.dtype),
            pltpu.VMEM(particles.shape, particles.dtype),
            pltpu.VMEM((half * PITCH, depth), jnp.float32),
            pltpu.VMEM((half, rows, depth), particles.dtype),
            pltpu.VMEM((cands, cycles, width), jnp.float32),
            pltpu.VMEM((half * (2 * cands + 4), depth), jnp.float32),
            pltpu.VMEM((rows // 128, 2 * cands * (half + 4), 128), jnp.float32),
            pltpu.VMEM((2 * cands * (half + 4), depth), jnp.float32),
            pltpu.VMEM((cands, rows), jnp.float32),
            pltpu.VMEM((n_grp, n_rep * message, width), jnp.float32),
            pltpu.VMEM((total, message, width), jnp.bfloat16),
            pltpu.VMEM((n_grp, 1, 128), jnp.float32),
        ]
        + [dma((total,))] * 8
        + [dma((rows // GROUP,)), dma((6,))],
        compiler_params=pltpu.CompilerParams(
            collective_id=0, has_side_effects=True, vmem_limit_bytes=LIMIT * 2**20
        ),
        name="em",
    )(
        *(
            pltpu.with_memory_space_constraint(array, pltpu.HBM)
            for array in (
                candidates,
                class_order.reshape(1, n_grp * owned),
                noise_var.reshape(1, rows),
                tables,
                references,
                particles,
            )
        )
    )
    height = owned * share
    chunks = 2 if height % 16 == 0 else 1
    class_sums, class_weights = pl.pallas_call(
        functools.partial(place_kernel, share),
        out_shape=(
            jax.ShapeDtypeStruct((height, width), jnp.float32),
            jax.ShapeDtypeStruct((1, owned), jnp.float32),
        ),
        in_specs=[vmem] * 3,
        out_specs=(hbm, vmem),
        scratch_shapes=[pltpu.VMEM((height, width), jnp.float32), dma((chunks,))],
        compiler_params=pltpu.CompilerParams(vmem_limit_bytes=16 * 2**20),
        name="place",
    )(back, weights, slots)
    return class_sums.reshape(owned, share, width), class_weights.reshape(owned)


def solution(mesh):
    placed = (
        P(("grp", "rep"), None, None),
        P(("grp", "rep")),
        P("grp", "rep", None),
        P(),
        P(("grp", "rep"), None),
    )
    return jax.shard_map(
        functools.partial(local, mesh.shape["grp"], mesh.shape["rep"]),
        mesh=mesh,
        in_specs=placed,
        out_specs=(P("grp", "rep", None), P("grp")),
        check_vma=False,
    )
```

```python
import functools
import math

import jax
import jax.numpy as jnp
import numpy as np
from jax import lax
from jax.experimental import pallas as pl
from jax.experimental.pallas import tpu as pltpu
from jax.sharding import PartitionSpec as P

GROUP = 16
PITCH = GROUP + 4
OWN = 2
LIMIT = 40


def angle_tables(freq_count, angle_count):
    product = np.arange(freq_count)[:, None] * np.arange(angle_count)[None, :] % angle_count
    phase_angle = product * (2.0 * math.pi / angle_count)
    return np.cos(phase_angle).astype(np.float32), np.sin(phase_angle).astype(np.float32)


def table_parts(table):
    high = table.astype(jnp.bfloat16)
    return high, (table - high.astype(np.float32)).astype(jnp.bfloat16)


def far_first(rep, n_rep, step):
    near = jnp.where(2 * rep < n_rep, rep, n_rep - 1 - rep)
    turn = step - (n_rep - 1 - 2 * near)
    inner = jnp.where(turn % 2 == 0, turn // 2, 2 * near - turn // 2)
    target = jnp.where(turn < 0, n_rep - 1 - step, inner)
    return jnp.where(2 * rep < n_rep, target, n_rep - 1 - target)


def each_peer(n_rep, n_grp, action):
    grp = lax.axis_index("grp")
    rep = lax.axis_index("rep")

    @pl.loop(0, n_rep)
    def _(step):
        to_rep = far_first(rep, n_rep, step)
        for ahead in range(n_grp - 1, -1, -1):
            to_grp = lax.rem(grp + ahead, n_grp)
            if ahead:
                action(to_grp, to_rep)
            else:

                @pl.when(to_rep != rep)
                def _():
                    action(to_grp, to_rep)


def peer_of(step, n_rep, total):
    me = lax.axis_index("grp") * n_rep + lax.axis_index("rep")
    peer = lax.rem(me + step, total)
    return peer, {"grp": peer // n_rep, "rep": lax.rem(peer, n_rep)}


def greet_all(n_rep, n_grp):
    barrier = pltpu.get_barrier_semaphore()

    def greet(to_grp, to_rep):
        pl.semaphore_signal(
            barrier,
            inc=1,
            device_id={"grp": to_grp, "rep": to_rep},
            device_id_type=pl.DeviceIdType.MESH,
        )

    each_peer(n_rep, n_grp, greet)


def await_all(total):
    pl.semaphore_wait(pltpu.get_barrier_semaphore(), total - 1)


def remote(src, dst, send_sem, recv_sem, where):
    return pltpu.make_async_remote_copy(
        src_ref=src,
        dst_ref=dst,
        send_sem=send_sem,
        recv_sem=recv_sem,
        device_id=where,
        device_id_type=pl.DeviceIdType.MESH,
    )


def split_wide(value):
    high = value.astype(jnp.bfloat16)
    return high, (value - high.astype(jnp.float32)).astype(jnp.bfloat16)


def dot_wide(left, right):
    return jnp.dot(left, right, preferred_element_type=jnp.float32)


def dot_parts(table_high, table_low, value):
    high, low = split_wide(value)
    return dot_wide(table_high, high) + dot_wide(table_low, high) + dot_wide(table_high, low)


def pass_kernel(
    n_rep,
    total,
    cand_hbm,
    order_hbm,
    noise_hbm,
    tables_hbm,
    refs_hbm,
    rows_ref,
    back_got,
    weight_got,
    slots_ref,
    cand_ref,
    order_ref,
    noise_ref,
    tables_ref,
    refs_ref,
    cand_pad,
    cand_all,
    slot_vec,
    slot_smem,
    send_buf,
    got_buf,
    in_buf,
    mid_buf,
    x_buf,
    chosen_buf,
    q_buf,
    f_buf,
    t_buf,
    norm_buf,
    turned_buf,
    back_send,
    weight_send,
    c_send,
    c_recv,
    d_send,
    d_recv,
    s_send,
    s_recv,
    w_send,
    w_recv,
    in_sem,
    l_sem,
):
    grp = lax.axis_index("grp")
    rep = lax.axis_index("rep")
    me = grp * n_rep + rep
    n_grp = total // n_rep
    owned, share, width = refs_ref.shape
    rows, cycles, _ = rows_ref.shape
    half = width // 2
    depth = 2 * cycles
    blocks = rows // GROUP
    cands = n_grp * OWN
    both = 2 * cands
    pitch = half + 4
    q_pitch = both + 4
    message = OWN * share

    def load(block):
        part = pl.ds(block * GROUP, GROUP)
        return pltpu.make_async_copy(rows_ref.at[part], in_buf.at[part], in_sem.at[block])

    pairs = (
        (cand_hbm, cand_ref),
        (order_hbm, order_ref),
        (refs_hbm, refs_ref),
        (noise_hbm, noise_ref),
        (tables_hbm, tables_ref),
    )
    reads = [
        pltpu.make_async_copy(src, dst, l_sem.at[n]) for n, (src, dst) in enumerate(pairs)
    ]
    reads[0].start()
    greet_all(n_rep, n_grp)
    for read in reads[1:3]:
        read.start()

    @pl.loop(0, blocks)
    def _(block):
        load(block).start()

    for read in reads[3:]:
        read.start()
    cand_pad[...] = jnp.full(cand_pad.shape, -1, jnp.int32)
    reads[0].wait()
    cand_pad[:, : cand_ref.shape[1]] = cand_ref[...]

    def relayout(start, stop):
        @pl.loop(start, stop)
        def _(block):
            load(block).wait()
            for p in range(GROUP):
                image = in_buf.at[block * GROUP + p]
                turned = jnp.concatenate([image[:, :half], image[:, half:]], axis=0).T
                mid_buf[pl.ds(p, half, stride=PITCH), :] = turned.astype(jnp.float32)
            part = pl.ds(pl.multiple_of(block * GROUP, GROUP), GROUP)
            for k in range(half):
                x_buf[k, part, :] = mid_buf[pl.ds(k * PITCH, GROUP), :].astype(x_buf.dtype)

    cut_one, cut_two = blocks // 4, blocks // 2
    relayout(0, cut_one)
    await_all(total)

    def cand_copy(to_grp, to_rep, slot):
        where = {"grp": to_grp, "rep": to_rep}
        peer = to_grp * n_rep + to_rep
        return remote(cand_pad, cand_all.at[slot], c_send.at[peer], c_recv.at[slot], where)

    each_peer(n_rep, n_grp, lambda g, r: cand_copy(g, r, me).start())

    cand_all[me] = cand_pad[...]
    relayout(cut_one, cut_two)

    @pl.loop(1, total)
    def _(step):
        peer, where = peer_of(step, n_rep, total)
        cand_copy(where["grp"], where["rep"], peer).wait_recv()

    reads[1].wait()
    reads[2].wait()
    order = order_ref[...]
    slot_no = lax.broadcasted_iota(jnp.int32, (1, order.shape[1]), 1) - grp * owned
    mine = jnp.where((slot_no >= 0) & (slot_no < owned), order, -2)
    wanted = cand_all[...].reshape(total, cand_all.shape[2])
    hit = wanted[:, 0:1] == mine
    for j in range(1, cand_ref.shape[1]):
        hit = jnp.logical_or(hit, wanted[:, j : j + 1] == mine)
    first = jnp.min(jnp.where(hit, slot_no, 2 * owned), axis=1, keepdims=True)
    last = jnp.max(jnp.where(hit, slot_no, -1), axis=1, keepdims=True)
    lane = lax.broadcasted_iota(jnp.int32, slot_vec.shape, 1)
    slot_vec[...] = jnp.where(
        lane == 0, jnp.minimum(first, owned - 1), jnp.maximum(last, 0)
    )
    to_scalar = pltpu.make_async_copy(slot_vec, slot_smem, l_sem.at[len(pairs)])
    to_scalar.start()
    to_scalar.wait()

    def data_copy(to_grp, to_rep, slot):
        where = {"grp": to_grp, "rep": to_rep}
        peer = to_grp * n_rep + to_rep
        return remote(
            send_buf.at[peer], got_buf.at[slot], d_send.at[peer], d_recv.at[slot], where
        )

    def give(to_grp, to_rep):
        peer = to_grp * n_rep + to_rep
        for i in range(OWN):
            send_buf[peer, i] = refs_ref[slot_smem[peer, i]]
        data_copy(to_grp, to_rep, me).start()

    each_peer(n_rep, n_grp, give)
    slots_ref[...] = jnp.where(lane == 0, first, last)

    for i in range(OWN):
        got_buf[me, i] = refs_ref[slot_smem[me, i]]

    relayout(cut_two, blocks)

    live = []
    if cands != cand_ref.shape[1]:
        held = cand_ref[:, 0:1] == order
        for j in range(1, cand_ref.shape[1]):
            held = jnp.logical_or(held, cand_ref[:, j : j + 1] == order)
        slot_all = lax.broadcasted_iota(jnp.int32, order.shape, 1)
        for g in range(n_grp):
            inside = held & (slot_all >= g * owned) & (slot_all < (g + 1) * owned)
            live.append(jnp.max(jnp.where(inside, 1.0, 0.0), axis=1, keepdims=True) > 0.0)

    @pl.loop(1, total)
    def _(step):
        peer, where = peer_of(step, n_rep, total)
        cand_copy(where["grp"], where["rep"], me).wait_send()
        data_copy(where["grp"], where["rep"], peer).wait()

    q_lane = lax.broadcasted_iota(jnp.int32, (half, depth), 1)
    for j in range(cands):
        g, i = j // OWN, j % OWN
        for r in range(n_rep):
            chosen_buf[j, pl.ds(r * share, share), :] = got_buf[g * n_rep + r, i].astype(
                jnp.float32
            )
        wide = chosen_buf[j]
        total_square = jnp.sum(jnp.sum(wide * wide, axis=0, keepdims=True), axis=1, keepdims=True)
        norm_buf[j : j + 1, :] = jnp.broadcast_to(0.5 * total_square, (1, rows))
        turned = jnp.concatenate([wide[:, :half], wide[:, half:]], axis=0).T
        q_buf[pl.ds(2 * j, half, stride=q_pitch), :] = turned
        rolled = pltpu.roll(turned, cycles, 1)
        q_buf[pl.ds(2 * j + 1, half, stride=q_pitch), :] = jnp.where(
            q_lane < cycles, -rolled, rolled
        )

    lanes = f_buf.shape[2]
    tiles = range(f_buf.shape[0])

    def spread(k):
        return pl.ds(k, both, stride=pitch)

    def take(part):
        return jnp.concatenate([f_buf[t, part, :] for t in tiles], axis=1)

    def put(part, value):
        for t in tiles:
            f_buf[t, part, :] = value[:, t * lanes : (t + 1) * lanes]

    quarter = half // 2

    def spread_folded(pair, parity):
        return pl.ds(parity * quarter + pair, both, stride=pitch)

    def folded(j, parity, c):
        return pl.ds((2 * j + c) * pitch + parity * quarter, quarter)

    def angle_half(j, upper):
        return pl.ds((2 * j + upper) * pitch, half)

    @pl.loop(0, quarter, unroll=4)
    def _(pair):
        for parity in range(2):
            k = 2 * pair + parity
            found = lax.dot_general(
                q_buf[pl.ds(k * q_pitch, both), :].astype(jnp.bfloat16),
                x_buf[k],
                (((1,), (1,)), ((), ())),
                preferred_element_type=jnp.float32,
            )
            put(spread_folded(pair, parity), found)

    reads[3].wait()
    reads[4].wait()
    inv_noise = 1.0 / noise_ref[...]
    top = jnp.full((1, rows), -jnp.inf, jnp.float32)
    for j in range(cands):
        even, odd = (
            dot_parts(
                tables_ref[2 * parity],
                tables_ref[2 * parity + 1],
                jnp.concatenate([take(folded(j, parity, c)) for c in range(2)], axis=0),
            )
            for parity in range(2)
        )
        for upper, correlation in enumerate((even + odd, even - odd)):
            logits = (correlation - norm_buf[j : j + 1, :]) * inv_noise
            if live:
                logits = jnp.where(live[j // OWN], logits, -jnp.inf)
            put(angle_half(j, upper), logits)
            top = jnp.maximum(top, jnp.max(logits, axis=0, keepdims=True))

    sums = []
    for j in range(cands):
        part_sum = 0.0
        for upper in range(2):
            exponent = jnp.exp(take(angle_half(j, upper)) - top)
            put(angle_half(j, upper), exponent)
            part_sum = part_sum + jnp.sum(exponent, axis=0, keepdims=True)
        sums.append(part_sum)
    inv_sum = 1.0 / sum(sums)
    w_lane = lax.broadcasted_iota(jnp.int32, (1, weight_send.shape[2]), 1)
    for g in range(n_grp):
        line = jnp.zeros(w_lane.shape, jnp.float32)
        for i in range(OWN):
            weight = jnp.sum(sums[g * OWN + i] * inv_sum, axis=1, keepdims=True)
            line = jnp.where(w_lane == i, weight, line)
        weight_send[g] = line

    def weight_copy(to_grp, to_rep, slot):
        where = {"grp": to_grp, "rep": to_rep}
        peer = to_grp * n_rep + to_rep
        return remote(
            weight_send.at[to_grp], weight_got.at[slot], w_send.at[peer], w_recv.at[slot], where
        )

    each_peer(n_rep, n_grp, lambda g, r: weight_copy(g, r, me).start())

    weight_got[me] = weight_send[grp]

    for j in range(cands):
        lower, upper = (take(angle_half(j, h)) * inv_sum for h in range(2))
        for parity, weights in enumerate((lower + upper, lower - upper)):
            result = dot_parts(
                tables_ref[4 + 2 * parity], tables_ref[5 + 2 * parity], weights
            )
            for c in range(2):
                put(folded(j, parity, c), result[c * quarter : (c + 1) * quarter])

    @pl.loop(0, quarter, unroll=4)
    def _(pair):
        for parity in range(2):
            k = 2 * pair + parity
            spectra = take(spread_folded(pair, parity)).astype(jnp.bfloat16)
            t_buf[spread(k), :] = dot_wide(spectra, x_buf[k])

    def back_copy(g, r, slot):
        where = {"grp": g, "rep": r}
        peer = g * n_rep + r
        return remote(
            back_send.at[peer], back_got.at[slot], s_send.at[peer], s_recv.at[slot], where
        )

    for d in range(n_grp):
        g = lax.rem(grp + d, n_grp)
        for i in range(OWN):
            base = (g * OWN + i) * 2 * pitch
            by_real = t_buf[pl.ds(base, half), :]
            by_imag = pltpu.roll(t_buf[pl.ds(base + pitch, half), :], cycles, 1)
            turned = (by_real + jnp.where(q_lane < cycles, -by_imag, by_imag)).T
            for c in range(2):
                for r in range(n_rep):
                    at = c * cycles + r * share
                    turned_buf[
                        d, pl.ds(r * message + i * share, share), c * half : (c + 1) * half
                    ] = turned[at : at + share]
        for r in range(n_rep):
            back_send[g * n_rep + r] = turned_buf[d, pl.ds(r * message, message), :].astype(
                back_send.dtype
            )

    each_peer(n_rep, n_grp, lambda g, r: back_copy(g, r, me).start())
    back_got[me] = back_send[me]

    @pl.loop(1, total)
    def _(step):
        peer, where = peer_of(step, n_rep, total)
        weight_copy(where["grp"], where["rep"], peer).wait()
        back_copy(where["grp"], where["rep"], peer).wait()


def place_kernel(
    share, back_ref, weight_ref, slots_ref, sums_hbm, class_weight_ref, sums_buf, out_sem
):
    total, message, width = back_ref.shape
    height = sums_buf.shape[0]
    owned = class_weight_ref.shape[1]
    chunks = out_sem.shape[0]
    shift = share.bit_length() - 1
    slots = slots_ref[...]
    member = lax.broadcasted_iota(jnp.int32, (total, total * message), 1)
    member = lax.shift_right_logical(member, shift)
    block_no = lax.broadcasted_iota(jnp.int32, (total, total * message), 0)
    of_member = jnp.zeros(member.shape, jnp.int32)
    for i in range(OWN):
        of_member = jnp.where(member == block_no * OWN + i, slots[:, i : i + 1], of_member)
    of_member = jnp.sum(of_member, axis=0, keepdims=True)
    if message % 16 == 0:
        back = back_ref[...].reshape(total * message, width)
    else:
        back = jnp.concatenate(
            [back_ref[b].astype(jnp.float32) for b in range(total)], axis=0
        ).astype(jnp.bfloat16)
    rows = height // chunks
    copies = []
    for chunk in range(chunks):
        part = pl.ds(chunk * rows, rows)
        row = lax.broadcasted_iota(jnp.int32, (rows, total * message), 0) + chunk * rows
        lane = lax.broadcasted_iota(jnp.int32, (rows, total * message), 1)
        fits = jnp.logical_and(
            lax.shift_right_logical(row, shift) == of_member,
            ((row ^ lane) & (share - 1)) == 0,
        )
        sums_buf[part, :] = dot_wide(jnp.where(fits, 1.0, 0.0).astype(jnp.bfloat16), back)
        copy = pltpu.make_async_copy(
            sums_buf.at[part], sums_hbm.at[part], out_sem.at[chunk]
        )
        copy.start()
        copies.append(copy)

    got_weight = weight_ref[...].reshape(total, weight_ref.shape[2])
    w_slot = lax.broadcasted_iota(jnp.int32, got_weight.shape, 1)
    placed = jnp.zeros(got_weight.shape, jnp.float32)
    for i in range(OWN):
        placed = placed + jnp.where(
            w_slot == slots[:, i : i + 1], got_weight[:, i : i + 1], 0.0
        )
    class_weight_ref[...] = jnp.sum(placed, axis=0, keepdims=True)[:, :owned]
    for copy in copies:
        copy.wait()


def local(n_grp, n_rep, particles, noise_var, references, class_order, candidates):
    total = n_grp * n_rep
    owned, share, width = references.shape
    rows, cycles, _ = particles.shape
    half = width // 2
    depth = 2 * cycles
    cands = n_grp * OWN
    message = OWN * share
    cosine, sine = angle_tables(half, width)
    cosine, sine = cosine[:, :half], sine[:, :half]
    parities = [slice(0, None, 2), slice(1, None, 2)]
    from_freqs = [np.concatenate([cosine[p].T, -sine[p].T], axis=1) for p in parities]
    to_freqs = [np.concatenate([cosine[p], sine[p]], axis=0) for p in parities]
    vmem = pl.BlockSpec(memory_space=pltpu.VMEM)
    dma = pltpu.SemaphoreType.DMA
    hbm = pl.BlockSpec(memory_space=pltpu.HBM)
    tables = jnp.stack([part for t in from_freqs + to_freqs for part in table_parts(t)])
    back, weights, slots = pl.pallas_call(
        functools.partial(pass_kernel, n_rep, total),
        out_shape=(
            jax.ShapeDtypeStruct((total, message, width), jnp.bfloat16),
            jax.ShapeDtypeStruct((total, 1, 128), jnp.float32),
            jax.ShapeDtypeStruct((total, 128), jnp.int32),
        ),
        in_specs=[hbm] * 6,
        out_specs=(vmem, vmem, vmem),
        scratch_shapes=[
            pltpu.VMEM(candidates.shape, jnp.int32),
            pltpu.VMEM((1, n_grp * owned), jnp.int32),
            pltpu.VMEM((1, rows), jnp.float32),
            pltpu.VMEM((8, half, half), jnp.bfloat16),
            pltpu.VMEM(references.shape, references.dtype),
            pltpu.VMEM((1, 128), jnp.int32),
            pltpu.VMEM((total, 1, 128), jnp.int32),
            pltpu.VMEM((total, 128), jnp.int32),
            pltpu.SMEM((total, 128), jnp.int32),
            pltpu.VMEM((total, OWN, share, width), references.dtype),
            pltpu.VMEM((total, OWN, share, width), references.dtype),
            pltpu.VMEM(particles.shape, particles.dtype),
            pltpu.VMEM((half * PITCH, depth), jnp.float32),
            pltpu.VMEM((half, rows, depth), particles.dtype),
            pltpu.VMEM((cands, cycles, width), jnp.float32),
            pltpu.VMEM((half * (2 * cands + 4), depth), jnp.float32),
            pltpu.VMEM((rows // 128, 2 * cands * (half + 4), 128), jnp.float32),
            pltpu.VMEM((2 * cands * (half + 4), depth), jnp.float32),
            pltpu.VMEM((cands, rows), jnp.float32),
            pltpu.VMEM((n_grp, n_rep * message, width), jnp.float32),
            pltpu.VMEM((total, message, width), jnp.bfloat16),
            pltpu.VMEM((n_grp, 1, 128), jnp.float32),
        ]
        + [dma((total,))] * 8
        + [dma((rows // GROUP,)), dma((6,))],
        compiler_params=pltpu.CompilerParams(
            collective_id=0, has_side_effects=True, vmem_limit_bytes=LIMIT * 2**20
        ),
        name="em",
    )(
        *(
            pltpu.with_memory_space_constraint(array, pltpu.HBM)
            for array in (
                candidates,
                class_order.reshape(1, n_grp * owned),
                noise_var.reshape(1, rows),
                tables,
                references,
                particles,
            )
        )
    )
    height = owned * share
    chunks = 2 if height % 16 == 0 else 1
    class_sums, class_weights = pl.pallas_call(
        functools.partial(place_kernel, share),
        out_shape=(
            jax.ShapeDtypeStruct((height, width), jnp.float32),
            jax.ShapeDtypeStruct((1, owned), jnp.float32),
        ),
        in_specs=[vmem] * 3,
        out_specs=(hbm, vmem),
        scratch_shapes=[pltpu.VMEM((height, width), jnp.float32), dma((chunks,))],
        compiler_params=pltpu.CompilerParams(vmem_limit_bytes=16 * 2**20),
        name="place",
    )(back, weights, slots)
    return class_sums.reshape(owned, share, width), class_weights.reshape(owned)


def solution(mesh):
    placed = (
        P(("grp", "rep"), None, None),
        P(("grp", "rep")),
        P("grp", "rep", None),
        P(),
        P(("grp", "rep"), None),
    )
    return jax.shard_map(
        functools.partial(local, mesh.shape["grp"], mesh.shape["rep"]),
        mesh=mesh,
        in_specs=placed,
        out_specs=(P("grp", "rep", None), P("grp")),
        check_vma=False,
    )
```

```python
import functools
import math

import jax
import jax.numpy as jnp
import numpy as np
from jax import lax
from jax.experimental import pallas as pl
from jax.experimental.pallas import tpu as pltpu
from jax.sharding import PartitionSpec as P

GROUP = 16
PITCH = GROUP + 4
OWN = 2
LIMIT = 40


def angle_tables(freq_count, angle_count):
    product = np.arange(freq_count)[:, None] * np.arange(angle_count)[None, :] % angle_count
    phase_angle = product * (2.0 * math.pi / angle_count)
    return np.cos(phase_angle).astype(np.float32), np.sin(phase_angle).astype(np.float32)


def table_parts(table):
    high = table.astype(jnp.bfloat16)
    return high, (table - high.astype(np.float32)).astype(jnp.bfloat16)


def far_first(rep, n_rep, step):
    near = jnp.where(2 * rep < n_rep, rep, n_rep - 1 - rep)
    turn = step - (n_rep - 1 - 2 * near)
    inner = jnp.where(turn % 2 == 0, turn // 2, 2 * near - turn // 2)
    target = jnp.where(turn < 0, n_rep - 1 - step, inner)
    return jnp.where(2 * rep < n_rep, target, n_rep - 1 - target)


def each_peer(n_rep, n_grp, action):
    grp = lax.axis_index("grp")
    rep = lax.axis_index("rep")

    @pl.loop(0, n_rep)
    def _(step):
        to_rep = far_first(rep, n_rep, step)
        for ahead in range(n_grp - 1, -1, -1):
            to_grp = lax.rem(grp + ahead, n_grp)
            if ahead:
                action(to_grp, to_rep)
            else:

                @pl.when(to_rep != rep)
                def _():
                    action(to_grp, to_rep)


def peer_of(step, n_rep, total):
    me = lax.axis_index("grp") * n_rep + lax.axis_index("rep")
    peer = lax.rem(me + step, total)
    return peer, {"grp": peer // n_rep, "rep": lax.rem(peer, n_rep)}


def greet_all(n_rep, n_grp):
    barrier = pltpu.get_barrier_semaphore()

    def greet(to_grp, to_rep):
        pl.semaphore_signal(
            barrier,
            inc=1,
            device_id={"grp": to_grp, "rep": to_rep},
            device_id_type=pl.DeviceIdType.MESH,
        )

    each_peer(n_rep, n_grp, greet)


def await_all(total):
    pl.semaphore_wait(pltpu.get_barrier_semaphore(), total - 1)


def remote(src, dst, send_sem, recv_sem, where):
    return pltpu.make_async_remote_copy(
        src_ref=src,
        dst_ref=dst,
        send_sem=send_sem,
        recv_sem=recv_sem,
        device_id=where,
        device_id_type=pl.DeviceIdType.MESH,
    )


def split_wide(value):
    high = value.astype(jnp.bfloat16)
    return high, (value - high.astype(jnp.float32)).astype(jnp.bfloat16)


def dot_wide(left, right):
    return jnp.dot(left, right, preferred_element_type=jnp.float32)


def dot_parts(table_high, table_low, value):
    high, low = split_wide(value)
    return dot_wide(table_high, high) + dot_wide(table_low, high) + dot_wide(table_high, low)


def pass_kernel(
    n_rep,
    total,
    cand_hbm,
    order_hbm,
    noise_hbm,
    tables_hbm,
    refs_hbm,
    rows_ref,
    back_got,
    weight_got,
    slots_ref,
    cand_ref,
    order_ref,
    noise_ref,
    tables_ref,
    refs_ref,
    cand_pad,
    cand_all,
    slot_vec,
    slot_smem,
    send_buf,
    got_buf,
    in_buf,
    mid_buf,
    x_buf,
    chosen_buf,
    q_buf,
    f_buf,
    t_buf,
    norm_buf,
    turned_buf,
    back_send,
    weight_send,
    c_send,
    c_recv,
    d_send,
    d_recv,
    s_send,
    s_recv,
    w_send,
    w_recv,
    in_sem,
    l_sem,
):
    grp = lax.axis_index("grp")
    rep = lax.axis_index("rep")
    me = grp * n_rep + rep
    n_grp = total // n_rep
    owned, share, width = refs_ref.shape
    rows, cycles, _ = rows_ref.shape
    half = width // 2
    depth = 2 * cycles
    blocks = rows // GROUP
    cands = n_grp * OWN
    both = 2 * cands
    pitch = half + 4
    q_pitch = both + 4
    message = OWN * share

    def load(block):
        part = pl.ds(block * GROUP, GROUP)
        return pltpu.make_async_copy(rows_ref.at[part], in_buf.at[part], in_sem.at[block])

    pairs = (
        (cand_hbm, cand_ref),
        (order_hbm, order_ref),
        (refs_hbm, refs_ref),
        (noise_hbm, noise_ref),
        (tables_hbm, tables_ref),
    )
    reads = [
        pltpu.make_async_copy(src, dst, l_sem.at[n]) for n, (src, dst) in enumerate(pairs)
    ]
    reads[0].start()
    greet_all(n_rep, n_grp)
    for read in reads[1:3]:
        read.start()

    @pl.loop(0, blocks)
    def _(block):
        load(block).start()

    for read in reads[3:]:
        read.start()
    cand_pad[...] = jnp.full(cand_pad.shape, -1, jnp.int32)
    reads[0].wait()
    cand_pad[:, : cand_ref.shape[1]] = cand_ref[...]

    def relayout(start, stop):
        @pl.loop(start, stop)
        def _(block):
            load(block).wait()
            for p in range(GROUP):
                image = in_buf.at[block * GROUP + p]
                turned = jnp.concatenate([image[:, :half], image[:, half:]], axis=0).T
                mid_buf[pl.ds(p, half, stride=PITCH), :] = turned.astype(jnp.float32)
            part = pl.ds(pl.multiple_of(block * GROUP, GROUP), GROUP)
            for k in range(half):
                x_buf[k, part, :] = mid_buf[pl.ds(k * PITCH, GROUP), :].astype(x_buf.dtype)

    cut_one, cut_two = blocks // 4, blocks // 2
    relayout(0, cut_one)
    await_all(total)

    def cand_copy(to_grp, to_rep, slot):
        where = {"grp": to_grp, "rep": to_rep}
        peer = to_grp * n_rep + to_rep
        return remote(cand_pad, cand_all.at[slot], c_send.at[peer], c_recv.at[slot], where)

    each_peer(n_rep, n_grp, lambda g, r: cand_copy(g, r, me).start())

    cand_all[me] = cand_pad[...]
    relayout(cut_one, cut_two)

    @pl.loop(1, total)
    def _(step):
        peer, where = peer_of(step, n_rep, total)
        cand_copy(where["grp"], where["rep"], peer).wait_recv()

    reads[1].wait()
    reads[2].wait()
    order = order_ref[...]
    slot_no = lax.broadcasted_iota(jnp.int32, (1, order.shape[1]), 1) - grp * owned
    mine = jnp.where((slot_no >= 0) & (slot_no < owned), order, -2)
    wanted = cand_all[...].reshape(total, cand_all.shape[2])
    hit = wanted[:, 0:1] == mine
    for j in range(1, cand_ref.shape[1]):
        hit = jnp.logical_or(hit, wanted[:, j : j + 1] == mine)
    first = jnp.min(jnp.where(hit, slot_no, 2 * owned), axis=1, keepdims=True)
    last = jnp.max(jnp.where(hit, slot_no, -1), axis=1, keepdims=True)
    lane = lax.broadcasted_iota(jnp.int32, slot_vec.shape, 1)
    slot_vec[...] = jnp.where(
        lane == 0, jnp.minimum(first, owned - 1), jnp.maximum(last, 0)
    )
    to_scalar = pltpu.make_async_copy(slot_vec, slot_smem, l_sem.at[len(pairs)])
    to_scalar.start()
    to_scalar.wait()

    def data_copy(to_grp, to_rep, slot):
        where = {"grp": to_grp, "rep": to_rep}
        peer = to_grp * n_rep + to_rep
        return remote(
            send_buf.at[peer], got_buf.at[slot], d_send.at[peer], d_recv.at[slot], where
        )

    def give(to_grp, to_rep):
        peer = to_grp * n_rep + to_rep
        for i in range(OWN):
            send_buf[peer, i] = refs_ref[slot_smem[peer, i]]
        data_copy(to_grp, to_rep, me).start()

    each_peer(n_rep, n_grp, give)
    slots_ref[...] = jnp.where(lane == 0, first, last)

    for i in range(OWN):
        got_buf[me, i] = refs_ref[slot_smem[me, i]]

    relayout(cut_two, blocks)

    live = []
    if cands != cand_ref.shape[1]:
        held = cand_ref[:, 0:1] == order
        for j in range(1, cand_ref.shape[1]):
            held = jnp.logical_or(held, cand_ref[:, j : j + 1] == order)
        slot_all = lax.broadcasted_iota(jnp.int32, order.shape, 1)
        for g in range(n_grp):
            inside = held & (slot_all >= g * owned) & (slot_all < (g + 1) * owned)
            live.append(jnp.max(jnp.where(inside, 1.0, 0.0), axis=1, keepdims=True) > 0.0)

    @pl.loop(1, total)
    def _(step):
        peer, where = peer_of(step, n_rep, total)
        cand_copy(where["grp"], where["rep"], me).wait_send()
        data_copy(where["grp"], where["rep"], peer).wait_send()

    @pl.loop(1, total)
    def _(step):
        peer, where = peer_of(step, n_rep, total)
        data_copy(where["grp"], where["rep"], peer).wait_recv()

    q_lane = lax.broadcasted_iota(jnp.int32, (half, depth), 1)
    for j in range(cands):
        g, i = j // OWN, j % OWN
        for r in range(n_rep):
            chosen_buf[j, pl.ds(r * share, share), :] = got_buf[g * n_rep + r, i].astype(
                jnp.float32
            )
        wide = chosen_buf[j]
        total_square = jnp.sum(jnp.sum(wide * wide, axis=0, keepdims=True), axis=1, keepdims=True)
        norm_buf[j : j + 1, :] = jnp.broadcast_to(0.5 * total_square, (1, rows))
        turned = jnp.concatenate([wide[:, :half], wide[:, half:]], axis=0).T
        q_buf[pl.ds(2 * j, half, stride=q_pitch), :] = turned
        rolled = pltpu.roll(turned, cycles, 1)
        q_buf[pl.ds(2 * j + 1, half, stride=q_pitch), :] = jnp.where(
            q_lane < cycles, -rolled, rolled
        )

    lanes = f_buf.shape[2]
    tiles = range(f_buf.shape[0])

    def spread(k):
        return pl.ds(k, both, stride=pitch)

    def take(part):
        return jnp.concatenate([f_buf[t, part, :] for t in tiles], axis=1)

    def put(part, value):
        for t in tiles:
            f_buf[t, part, :] = value[:, t * lanes : (t + 1) * lanes]

    quarter = half // 2

    def spread_folded(pair, parity):
        return pl.ds(parity * quarter + pair, both, stride=pitch)

    def folded(j, parity, c):
        return pl.ds((2 * j + c) * pitch + parity * quarter, quarter)

    def angle_half(j, upper):
        return pl.ds((2 * j + upper) * pitch, half)

    @pl.loop(0, quarter, unroll=4)
    def _(pair):
        for parity in range(2):
            k = 2 * pair + parity
            found = lax.dot_general(
                q_buf[pl.ds(k * q_pitch, both), :].astype(jnp.bfloat16),
                x_buf[k],
                (((1,), (1,)), ((), ())),
                preferred_element_type=jnp.float32,
            )
            put(spread_folded(pair, parity), found)

    reads[3].wait()
    reads[4].wait()
    inv_noise = 1.0 / noise_ref[...]
    top = jnp.full((1, rows), -jnp.inf, jnp.float32)
    for j in range(cands):
        even, odd = (
            dot_parts(
                tables_ref[2 * parity],
                tables_ref[2 * parity + 1],
                jnp.concatenate([take(folded(j, parity, c)) for c in range(2)], axis=0),
            )
            for parity in range(2)
        )
        for upper, correlation in enumerate((even + odd, even - odd)):
            logits = (correlation - norm_buf[j : j + 1, :]) * inv_noise
            if live:
                logits = jnp.where(live[j // OWN], logits, -jnp.inf)
            put(angle_half(j, upper), logits)
            top = jnp.maximum(top, jnp.max(logits, axis=0, keepdims=True))

    sums = []
    for j in range(cands):
        part_sum = 0.0
        for upper in range(2):
            exponent = jnp.exp(take(angle_half(j, upper)) - top)
            put(angle_half(j, upper), exponent)
            part_sum = part_sum + jnp.sum(exponent, axis=0, keepdims=True)
        sums.append(part_sum)
    inv_sum = 1.0 / sum(sums)
    w_lane = lax.broadcasted_iota(jnp.int32, (1, weight_send.shape[2]), 1)
    for g in range(n_grp):
        line = jnp.zeros(w_lane.shape, jnp.float32)
        for i in range(OWN):
            weight = jnp.sum(sums[g * OWN + i] * inv_sum, axis=1, keepdims=True)
            line = jnp.where(w_lane == i, weight, line)
        weight_send[g] = line

    def weight_copy(to_grp, to_rep, slot):
        where = {"grp": to_grp, "rep": to_rep}
        peer = to_grp * n_rep + to_rep
        return remote(
            weight_send.at[to_grp], weight_got.at[slot], w_send.at[peer], w_recv.at[slot], where
        )

    each_peer(n_rep, n_grp, lambda g, r: weight_copy(g, r, me).start())

    weight_got[me] = weight_send[grp]

    for j in range(cands):
        lower, upper = (take(angle_half(j, h)) * inv_sum for h in range(2))
        for parity, weights in enumerate((lower + upper, lower - upper)):
            result = dot_parts(
                tables_ref[4 + 2 * parity], tables_ref[5 + 2 * parity], weights
            )
            for c in range(2):
                put(folded(j, parity, c), result[c * quarter : (c + 1) * quarter])

    @pl.loop(0, quarter, unroll=4)
    def _(pair):
        for parity in range(2):
            k = 2 * pair + parity
            spectra = take(spread_folded(pair, parity)).astype(jnp.bfloat16)
            t_buf[spread(k), :] = dot_wide(spectra, x_buf[k])

    def back_copy(g, r, slot):
        where = {"grp": g, "rep": r}
        peer = g * n_rep + r
        return remote(
            back_send.at[peer], back_got.at[slot], s_send.at[peer], s_recv.at[slot], where
        )

    for d in range(n_grp):
        g = lax.rem(grp + d, n_grp)
        for i in range(OWN):
            base = (g * OWN + i) * 2 * pitch
            by_real = t_buf[pl.ds(base, half), :]
            by_imag = pltpu.roll(t_buf[pl.ds(base + pitch, half), :], cycles, 1)
            turned = (by_real + jnp.where(q_lane < cycles, -by_imag, by_imag)).T
            for c in range(2):
                for r in range(n_rep):
                    at = c * cycles + r * share
                    turned_buf[
                        d, pl.ds(r * message + i * share, share), c * half : (c + 1) * half
                    ] = turned[at : at + share]
        for r in range(n_rep):
            back_send[g * n_rep + r] = turned_buf[d, pl.ds(r * message, message), :].astype(
                back_send.dtype
            )

    each_peer(n_rep, n_grp, lambda g, r: back_copy(g, r, me).start())
    back_got[me] = back_send[me]

    @pl.loop(1, total)
    def _(step):
        peer, where = peer_of(step, n_rep, total)
        weight_copy(where["grp"], where["rep"], peer).wait()
        back_copy(where["grp"], where["rep"], peer).wait_send()

    @pl.loop(1, total)
    def _(step):
        peer, where = peer_of(step, n_rep, total)
        back_copy(where["grp"], where["rep"], peer).wait_recv()


def place_kernel(
    share, back_ref, weight_ref, slots_ref, sums_hbm, class_weight_ref, sums_buf, out_sem
):
    total, message, width = back_ref.shape
    height = sums_buf.shape[0]
    owned = class_weight_ref.shape[1]
    chunks = out_sem.shape[0]
    shift = share.bit_length() - 1
    slots = slots_ref[...]
    member = lax.broadcasted_iota(jnp.int32, (total, total * message), 1)
    member = lax.shift_right_logical(member, shift)
    block_no = lax.broadcasted_iota(jnp.int32, (total, total * message), 0)
    of_member = jnp.zeros(member.shape, jnp.int32)
    for i in range(OWN):
        of_member = jnp.where(member == block_no * OWN + i, slots[:, i : i + 1], of_member)
    of_member = jnp.sum(of_member, axis=0, keepdims=True)
    if message % 16 == 0:
        back = back_ref[...].reshape(total * message, width)
    else:
        back = jnp.concatenate(
            [back_ref[b].astype(jnp.float32) for b in range(total)], axis=0
        ).astype(jnp.bfloat16)
    rows = height // chunks
    copies = []
    for chunk in range(chunks):
        part = pl.ds(chunk * rows, rows)
        row = lax.broadcasted_iota(jnp.int32, (rows, total * message), 0) + chunk * rows
        lane = lax.broadcasted_iota(jnp.int32, (rows, total * message), 1)
        fits = jnp.logical_and(
            lax.shift_right_logical(row, shift) == of_member,
            ((row ^ lane) & (share - 1)) == 0,
        )
        sums_buf[part, :] = dot_wide(jnp.where(fits, 1.0, 0.0).astype(jnp.bfloat16), back)
        copy = pltpu.make_async_copy(
            sums_buf.at[part], sums_hbm.at[part], out_sem.at[chunk]
        )
        copy.start()
        copies.append(copy)

    got_weight = weight_ref[...].reshape(total, weight_ref.shape[2])
    w_slot = lax.broadcasted_iota(jnp.int32, got_weight.shape, 1)
    placed = jnp.zeros(got_weight.shape, jnp.float32)
    for i in range(OWN):
        placed = placed + jnp.where(
            w_slot == slots[:, i : i + 1], got_weight[:, i : i + 1], 0.0
        )
    class_weight_ref[...] = jnp.sum(placed, axis=0, keepdims=True)[:, :owned]
    for copy in copies:
        copy.wait()


def local(n_grp, n_rep, particles, noise_var, references, class_order, candidates):
    total = n_grp * n_rep
    owned, share, width = references.shape
    rows, cycles, _ = particles.shape
    half = width // 2
    depth = 2 * cycles
    cands = n_grp * OWN
    message = OWN * share
    cosine, sine = angle_tables(half, width)
    cosine, sine = cosine[:, :half], sine[:, :half]
    parities = [slice(0, None, 2), slice(1, None, 2)]
    from_freqs = [np.concatenate([cosine[p].T, -sine[p].T], axis=1) for p in parities]
    to_freqs = [np.concatenate([cosine[p], sine[p]], axis=0) for p in parities]
    vmem = pl.BlockSpec(memory_space=pltpu.VMEM)
    dma = pltpu.SemaphoreType.DMA
    hbm = pl.BlockSpec(memory_space=pltpu.HBM)
    tables = jnp.stack([part for t in from_freqs + to_freqs for part in table_parts(t)])
    back, weights, slots = pl.pallas_call(
        functools.partial(pass_kernel, n_rep, total),
        out_shape=(
            jax.ShapeDtypeStruct((total, message, width), jnp.bfloat16),
            jax.ShapeDtypeStruct((total, 1, 128), jnp.float32),
            jax.ShapeDtypeStruct((total, 128), jnp.int32),
        ),
        in_specs=[hbm] * 6,
        out_specs=(vmem, vmem, vmem),
        scratch_shapes=[
            pltpu.VMEM(candidates.shape, jnp.int32),
            pltpu.VMEM((1, n_grp * owned), jnp.int32),
            pltpu.VMEM((1, rows), jnp.float32),
            pltpu.VMEM((8, half, half), jnp.bfloat16),
            pltpu.VMEM(references.shape, references.dtype),
            pltpu.VMEM((1, 128), jnp.int32),
            pltpu.VMEM((total, 1, 128), jnp.int32),
            pltpu.VMEM((total, 128), jnp.int32),
            pltpu.SMEM((total, 128), jnp.int32),
            pltpu.VMEM((total, OWN, share, width), references.dtype),
            pltpu.VMEM((total, OWN, share, width), references.dtype),
            pltpu.VMEM(particles.shape, particles.dtype),
            pltpu.VMEM((half * PITCH, depth), jnp.float32),
            pltpu.VMEM((half, rows, depth), particles.dtype),
            pltpu.VMEM((cands, cycles, width), jnp.float32),
            pltpu.VMEM((half * (2 * cands + 4), depth), jnp.float32),
            pltpu.VMEM((rows // 128, 2 * cands * (half + 4), 128), jnp.float32),
            pltpu.VMEM((2 * cands * (half + 4), depth), jnp.float32),
            pltpu.VMEM((cands, rows), jnp.float32),
            pltpu.VMEM((n_grp, n_rep * message, width), jnp.float32),
            pltpu.VMEM((total, message, width), jnp.bfloat16),
            pltpu.VMEM((n_grp, 1, 128), jnp.float32),
        ]
        + [dma((total,))] * 8
        + [dma((rows // GROUP,)), dma((6,))],
        compiler_params=pltpu.CompilerParams(
            collective_id=0, has_side_effects=True, vmem_limit_bytes=LIMIT * 2**20
        ),
        name="em",
    )(
        *(
            pltpu.with_memory_space_constraint(array, pltpu.HBM)
            for array in (
                candidates,
                class_order.reshape(1, n_grp * owned),
                noise_var.reshape(1, rows),
                tables,
                references,
                particles,
            )
        )
    )
    height = owned * share
    chunks = 2 if height % 16 == 0 else 1
    class_sums, class_weights = pl.pallas_call(
        functools.partial(place_kernel, share),
        out_shape=(
            jax.ShapeDtypeStruct((height, width), jnp.float32),
            jax.ShapeDtypeStruct((1, owned), jnp.float32),
        ),
        in_specs=[vmem] * 3,
        out_specs=(hbm, vmem),
        scratch_shapes=[pltpu.VMEM((height, width), jnp.float32), dma((chunks,))],
        compiler_params=pltpu.CompilerParams(vmem_limit_bytes=16 * 2**20),
        name="place",
    )(back, weights, slots)
    return class_sums.reshape(owned, share, width), class_weights.reshape(owned)


def solution(mesh):
    placed = (
        P(("grp", "rep"), None, None),
        P(("grp", "rep")),
        P("grp", "rep", None),
        P(),
        P(("grp", "rep"), None),
    )
    return jax.shard_map(
        functools.partial(local, mesh.shape["grp"], mesh.shape["rep"]),
        mesh=mesh,
        in_specs=placed,
        out_specs=(P("grp", "rep", None), P("grp")),
        check_vma=False,
    )
```
